256 devices in a mesh: band: 16 (over z_lo, y, core), section: 16 (over z_hi, x).
Axes of the slice: x: 4, y: 4, z: 8 (z_hi: 4, z_lo: 2; z = z_hi * 2 + z_lo), core: 2. Of those that a mesh axis runs over, the one named last changes fastest.
Arguments:
- fields: bfloat16 [4, 64, 128, 256], P(None, 'band'), may hold values from -6 to 6
- cotangent: bfloat16 [4, 64, 128, 256], P(None, 'band'), may hold values from -6 to 6
- kernels: bfloat16 [16, 3, 3, 256, 256], P('section'), may hold values from -0.0625 to 0.0625
- biases: float32 [16, 256], P('section'), may hold values from -2 to 2
Outputs:
- block_states: bfloat16 [16, 4, 64, 128, 256], P('section', None, 'band')
- field_grads: bfloat16 [16, 4, 64, 128, 256], P('section', None, 'band')
The draws below stay inside these ranges and needn't reach their ends.
All inputs are finite; a program needn't handle non-finite values.
Results may differ from the reference program's by a relative error of at most 0.023.
Values may be sent and summed in bfloat16 or wider, within the bound.
No kernel may reach another device: no remote copies, remote signals or barrier semaphores. Data moves between devices by JAX's collectives and lax.ppermute only.
A program may use at most 64 MiB of HBM per device.

```python
import jax
import jax.numpy as jnp
from jax import lax

C = 256
LON = 128
MICRO = 4
LAT = 64
SECTIONS = 16


def block_scale(key, extent, pieces, smallest, largest):
    factor_of, own = 1.0, jax.random.fold_in(key, 6)
    for dim, shards_of in pieces:
        steps = jnp.exp(jax.random.uniform(jax.random.fold_in(own, dim), (shards_of,), jnp.float32, smallest / len(pieces), largest / len(pieces)))
        factor_of = factor_of * jnp.repeat(steps, extent[dim] // shards_of).reshape([-1 if axis == dim else 1 for axis in range(len(extent))])
    return factor_of


def gaussian(stream_key, shape, width, bound, shards=(), dtype=jnp.bfloat16):
    loudness = block_scale(stream_key, shape, shards, -0.22, 0.18) if shards else 1.0
    values = jax.random.normal(stream_key, shape, jnp.float32) * width * loudness
    return jnp.minimum(jnp.maximum(values, -bound), bound).astype(dtype)


def setup_inputs(seed: int = 0) -> dict:
    arg_keys = jax.random.split(jax.random.key(seed), 5)
    fields = gaussian(arg_keys[0], (MICRO, LAT, LON, C), 1.0, 6.0, ((1, 16),))
    cotangent = gaussian(arg_keys[1], (MICRO, LAT, LON, C), 1.0, 6.0, ((1, 16),))
    kernels = gaussian(arg_keys[2], (SECTIONS, 3, 3, C, C), (36 * C) ** -0.5, 0.0625, ((0, 16),))
    biases = gaussian(arg_keys[3], (SECTIONS, C), 0.3, 2.0, ((0, 16),), jnp.float32)
    return dict(fields=fields, cotangent=cotangent, kernels=kernels, biases=biases)


def pole_pad(field, half_turn):
    north = jnp.roll(field[..., :1, :, :], half_turn, axis=-2)
    south = jnp.roll(field[..., -1:, :, :], half_turn, axis=-2)
    return jnp.concatenate([north, field, south], axis=-3)


def convolve(padded, kernel, offset):
    height = padded.shape[-3] - 2
    channels = padded.shape[-1]
    out_shape = padded.shape[:-3] + (height, padded.shape[-2], channels)
    summed = jnp.zeros(out_shape, jnp.float32)
    for col_off in range(3):
        rolled = jnp.roll(padded, 1 - col_off, axis=-2)
        for row_off in range(3):
            window = rolled[..., row_off:row_off + height, :, :].reshape(-1, channels)
            summed = summed + jnp.dot(window, kernel[row_off, col_off], preferred_element_type=jnp.float32).reshape(out_shape)
    return summed + offset.astype(jnp.float32)


def transpose_conv(delta_rows, kernel):
    channels = delta_rows.shape[-1]
    leading = delta_rows.ndim - 3
    flattened = delta_rows.reshape(-1, channels)
    summed = None
    for row_off in range(3):
        row_sum = jnp.zeros(delta_rows.shape, jnp.float32)
        for col_off in range(3):
            returned = lax.dot_general(flattened, kernel[row_off, col_off], (((1,), (1,)), ((), ())), preferred_element_type=jnp.float32).reshape(delta_rows.shape)
            row_sum = row_sum + jnp.roll(returned, col_off - 1, axis=-2)
        pad_widths = [(0, 0)] * leading + [(row_off, 2 - row_off), (0, 0), (0, 0)]
        padded_sum = jnp.pad(row_sum, pad_widths)
        summed = padded_sum if summed is None else summed + padded_sum
    return summed


def silu_slope(preact):
    sigmoid_v = jax.nn.sigmoid(preact)
    return sigmoid_v * (1.0 + preact * (1.0 - sigmoid_v))


def reference(fields, cotangent, kernels, biases):
    half_turn = LON // 2
    current = fields
    inputs_list = []
    states_list = []
    for section_index in range(SECTIONS):
        padded = pole_pad(current, half_turn)
        inputs_list.append(padded)
        preact = convolve(padded, kernels[section_index], biases[section_index])
        current = (current.astype(jnp.float32) + jax.nn.silu(preact)).astype(jnp.bfloat16)
        states_list.append(current)
    upstream = cotangent
    grads_list = [None] * SECTIONS
    for section_index in reversed(range(SECTIONS)):
        preact = convolve(inputs_list[section_index], kernels[section_index], biases[section_index])
        delta_rows = (upstream.astype(jnp.float32) * silu_slope(preact)).astype(jnp.bfloat16)
        spread = transpose_conv(delta_rows, kernels[section_index])
        summed = upstream.astype(jnp.float32) + spread[..., 1:-1, :, :]
        summed = summed.at[..., 0, :, :].add(jnp.roll(spread[..., 0, :, :], half_turn, axis=-2))
        summed = summed.at[..., -1, :, :].add(jnp.roll(spread[..., -1, :, :], half_turn, axis=-2))
        upstream = summed.astype(jnp.bfloat16)
        grads_list[section_index] = upstream
    return jnp.stack(states_list), jnp.stack(grads_list)
```

```python
import jax
import jax.numpy as jnp
from jax import lax
from jax.experimental import pallas as pl
from jax.experimental.pallas import tpu as pltpu
from jax.sharding import PartitionSpec as P


DEPTH = 4
BF16 = jnp.bfloat16
F32 = jnp.float32


def spread_columns(ref, base, value, shift, across, channels):
    count = value.shape[0]
    cells = value.reshape(count // across, across, channels)
    before = pltpu.roll(cells, shift % across, 1).reshape(count, channels)
    after = pltpu.roll(cells, -shift % across, 1).reshape(count, channels)
    ref[pl.ds(base, count), 0:channels] = before.astype(BF16)
    ref[pl.ds(base, count), channels : 2 * channels] = value.astype(BF16)
    ref[pl.ds(base, count), 2 * channels : 3 * channels] = after.astype(BF16)


def copy_weights(mine, theirs, weights, sems, parity, half):
    copies = []
    for layer in range(DEPTH):
        pair = []
        for side, source in enumerate((mine, theirs)):
            place = parity if side == 0 else 1 - parity
            pair.append(
                pltpu.make_async_copy(
                    source.at[layer, pl.ds(0, half)],
                    weights.at[layer, pl.ds(pl.multiple_of(place * half, 128), half)],
                    sems.at[layer, side],
                )
            )
        copies.append(pair)
    return copies


def forward_kernel(flags, own, above, below, mine, theirs, offsets, states, slopes_near, slopes_mid, slopes_far,
                   wide, weights, sems):
    rows, across, channels = own.shape
    is_first = flags[0] == 1
    is_last = flags[1] == 1
    half = weights.shape[1] // 2
    copies = copy_weights(mine, theirs, weights, sems, flags[2], half)
    for pair in copies:
        for copy in pair:
            copy.start()
    step = 2 * across
    for part, piece in enumerate((above, own, below)):
        for pair in range(rows // 2):
            value = piece[2 * pair : 2 * pair + 2].reshape(step, channels).astype(F32)
            spread_columns(wide, (part * rows + 2 * pair) * across, value, 1, across, channels)

    def poles():
        middle = across // 2
        top, bottom = rows * across, (2 * rows - 1) * across

        @pl.when(is_first)
        def _():
            wide[top - across : top - middle, :] = wide[top + middle : top + across, :]
            wide[top - middle : top, :] = wide[top : top + middle, :]

        @pl.when(is_last)
        def _():
            wide[bottom + across : bottom + across + middle, :] = wide[bottom + middle : bottom + across, :]
            wide[bottom + across + middle : bottom + 2 * across, :] = wide[bottom : bottom + middle, :]

    for layer in range(DEPTH):
        poles()
        for copy in copies[layer]:
            copy.wait()
        reach = DEPTH - 1 - layer
        offset = offsets[layer : layer + 1, :]
        first, last = rows - reach, 2 * rows + reach
        carry = []
        for row in range(first, last, 2):
            base = row * across
            preact = None
            for tap in range(3):
                term = jnp.dot(
                    wide[base + (tap - 1) * across : base + (tap - 1) * across + step, :],
                    weights[layer, tap * 3 * channels : (tap + 1) * 3 * channels, :],
                    preferred_element_type=F32,
                )
                preact = term if preact is None else preact + term
            preact = preact + offset
            sigmoid = 0.5 * jnp.tanh(0.5 * preact) + 0.5
            silu = preact * sigmoid
            slope = (sigmoid * (1.0 + preact * (1.0 - sigmoid))).astype(BF16)
            current = wide[base : base + step, channels : 2 * channels].astype(F32)
            result = (current + silu).astype(BF16)
            carry.append((row, result))
            for index in range(2):
                at = row + index
                line = slope[index * across : (index + 1) * across]
                if layer == 0 and rows - 1 <= at < 2 * rows + 1:
                    slopes_near[at - (rows - 1)] = line
                if layer == 1 and rows - 2 <= at < 2 * rows + 2:
                    slopes_mid[at - (rows - 2)] = line
                if layer >= 2 and rows <= at < 2 * rows:
                    slopes_far[layer - 2, at - rows] = line
                if rows <= at < 2 * rows:
                    states[layer, at - rows] = result[index * across : (index + 1) * across]
            if layer < DEPTH - 1 and len(carry) > 1:
                at, value = carry[-2]
                spread_columns(wide, at * across, value.astype(F32), 1, across, channels)
        if layer < DEPTH - 1:
            at, value = carry[-1]
            spread_columns(wide, at * across, value.astype(F32), 1, across, channels)


def backward_kernel(flags, own, above, below, slopes_near, slopes_mid, slopes_far, slopes_above, slopes_below,
                    mine, theirs, grads, upstream, wide, poles, weights, sems):
    rows, across, channels = own.shape
    is_first = flags[0] == 1
    is_last = flags[1] == 1
    half = weights.shape[1] // 2
    copies = copy_weights(mine, theirs, weights, sems, flags[2], half)
    for layer in reversed(range(DEPTH)):
        for copy in copies[layer]:
            copy.start()
    step = 2 * across
    for part, piece in enumerate((above, own, below)):
        upstream[part * rows : (part + 1) * rows] = piece[...]
    poles[...] = jnp.zeros(poles.shape, F32)
    contract = (((1,), (1,)), ((), ()))

    def slope_at(layer, row):
        if layer == 0:
            return slopes_near[row - (rows - 1)]
        if layer == 1:
            return slopes_mid[row - (rows - 2)]
        part, index = divmod(row, rows)
        return (slopes_above, slopes_far, slopes_below)[part][layer - 2, index]

    def tap_weight(layer, tap, column):
        at = (tap * 3 + column) * channels
        return weights[layer, at : at + channels, :]

    for layer in reversed(range(DEPTH)):
        reach = layer + 1
        for row in range(rows - reach, 2 * rows + reach):
            delta = upstream[row].astype(F32) * slope_at(layer, row).astype(F32)
            delta = delta.astype(BF16).astype(F32)
            spread_columns(wide, row * across, delta, -1, across, channels)
        top, bottom, middle = rows * across, (2 * rows - 1) * across, across // 2
        for copy in copies[layer]:
            copy.wait()

        def edge_terms(slot, base, tap):
            for piece in range(2):
                start = base + (1 - piece) * middle
                total = None
                for column in range(3):
                    term = lax.dot_general(
                        wide[start : start + middle, column * channels : (column + 1) * channels],
                        tap_weight(layer, tap, column), contract, preferred_element_type=F32,
                    )
                    total = term if total is None else total + term
                poles[slot, piece * middle : (piece + 1) * middle, :] = total

        @pl.when(is_first)
        def _():
            wide[top - across : top, :] = jnp.zeros((across, 3 * channels), BF16)
            edge_terms(0, top, 0)

        @pl.when(is_last)
        def _():
            wide[bottom + across : bottom + 2 * across, :] = jnp.zeros((across, 3 * channels), BF16)
            edge_terms(1, bottom, 2)

        for row in range(rows - layer, 2 * rows + layer, 2):
            base = row * across
            total = upstream[row : row + 2].reshape(step, channels).astype(F32)
            for tap in range(3):
                for column in range(3):
                    start = base + (1 - tap) * across
                    total = total + lax.dot_general(
                        wide[start : start + step, column * channels : (column + 1) * channels],
                        tap_weight(layer, tap, column), contract, preferred_element_type=F32,
                    )
            for index in range(2):
                at = row + index
                line = total[index * across : (index + 1) * across]
                if at == rows:
                    line = line + poles[0]
                if at == 2 * rows - 1:
                    line = line + poles[1]
                line = line.astype(BF16)
                upstream[at] = line
                if rows <= at < 2 * rows:
                    grads[layer, at - rows] = line


def shift(block, axis, pairs):
    return lax.ppermute(block, axis, pairs)


def on_device(fields, cotangent, kernels, biases):
    band_count = lax.axis_size("band")
    section_count = lax.axis_size("section")
    micro_count, rows, across, channels = fields.shape
    groups = section_count // DEPTH
    band = lax.axis_index("band")
    section = lax.axis_index("section")
    group = section // DEPTH
    place = section % DEPTH
    parity = band % 2
    flags = jnp.stack([band == 0, band == band_count - 1, parity == 1]).astype(jnp.int32)

    half = 9 * channels // 2
    bias = biases[0]
    high = lax.reduce_precision(bias, 8, 7)
    middle = lax.reduce_precision(bias - high, 8, 7)
    low = bias - high - middle
    extra = jnp.stack([high, middle, low] + [jnp.zeros_like(bias)] * 5).astype(BF16)
    own_half = lax.dynamic_slice_in_dim(kernels.reshape(9 * channels, channels), parity * half, half, 0)
    piece = jnp.concatenate([own_half, extra], axis=0)
    across_groups = [[g * DEPTH + p for g in range(groups)] for p in range(DEPTH)]
    in_group = [[g * DEPTH + p for p in range(DEPTH)] for g in range(groups)]
    partner = [(i, i ^ 1) for i in range(band_count)]
    by_group = lax.all_gather(piece, "section", axis_index_groups=across_groups)
    mine, theirs, offsets = [], [], []
    for g in range(groups):
        gathered = lax.all_gather(by_group[g], "section", axis_index_groups=in_group)
        mine.append(gathered)
        theirs.append(shift(gathered, "band", partner))
        parts = gathered[:, half : half + 3, :].astype(F32)
        offsets.append((parts[:, 0] + parts[:, 1]) + parts[:, 2])

    down = [(i, i + 1) for i in range(band_count - 1)]
    up = [(i + 1, i) for i in range(band_count - 1)]

    def edges(block):
        return shift(block, "band", down), shift(block, "band", up)

    row_shape = (rows, across, channels)
    smem = pl.BlockSpec(memory_space=pltpu.SMEM)
    vmem = pl.BlockSpec(memory_space=pltpu.VMEM)
    hbm = pl.BlockSpec(memory_space=pl.ANY)
    wide = pltpu.VMEM((3 * rows * across, 3 * channels), BF16)
    weight_room = pltpu.VMEM((DEPTH, 9 * channels, channels), BF16)
    sems = pltpu.SemaphoreType.DMA((DEPTH, 2))
    params = pltpu.CompilerParams(vmem_limit_bytes=48 * 1024 * 1024)

    def shaped(*shape):
        return jax.ShapeDtypeStruct(shape, BF16)

    current = lax.dynamic_index_in_dim(fields, place, 0, keepdims=False)
    all_states, slopes = [], []
    for g in range(groups):
        above, below = edges(current)
        states, near, mid, far = pl.pallas_call(
            forward_kernel,
            out_shape=(
                shaped(DEPTH, *row_shape),
                shaped(rows + 2, across, channels),
                shaped(rows + 4, across, channels),
                shaped(2, *row_shape),
            ),
            in_specs=[smem, vmem, vmem, vmem, hbm, hbm, vmem],
            out_specs=(vmem, vmem, vmem, vmem),
            scratch_shapes=[wide, weight_room, sems],
            compiler_params=params,
            name="forward",
        )(flags, current, above, below, mine[g], theirs[g], offsets[g])
        current = states[DEPTH - 1]
        all_states.append(states)
        slopes.append((near, mid, far) + edges(far))

    upstream = lax.dynamic_index_in_dim(cotangent, place, 0, keepdims=False)
    all_grads = [None] * groups
    for g in reversed(range(groups)):
        above, below = edges(upstream)
        grads = pl.pallas_call(
            backward_kernel,
            out_shape=shaped(DEPTH, *row_shape),
            in_specs=[smem] + [vmem] * 8 + [hbm, hbm],
            out_specs=vmem,
            scratch_shapes=[
                pltpu.VMEM((3 * rows, across, channels), BF16),
                wide,
                pltpu.VMEM((2, across, channels), F32),
                weight_room,
                sems,
            ],
            compiler_params=params,
            name="backward",
        )(flags, upstream, above, below, *slopes[g], mine[g], theirs[g])
        upstream = grads[0]
        all_grads[g] = grads

    def deliver(blocks):
        kept = lax.select_n(group, *blocks)
        out = jnp.zeros((micro_count,) + row_shape, BF16)
        out = lax.dynamic_update_index_in_dim(out, lax.dynamic_index_in_dim(kept, place, 0, keepdims=False), place, 0)
        for step in range(1, DEPTH):
            send = lax.dynamic_index_in_dim(kept, (place + step) % DEPTH, 0, keepdims=False)
            pairs = [(g * DEPTH + p, g * DEPTH + (p + step) % DEPTH) for g in range(groups) for p in range(DEPTH)]
            received = shift(send, "section", pairs)
            out = lax.dynamic_update_index_in_dim(out, received, (place - step) % DEPTH, 0)
        return out[None]

    return deliver(all_states), deliver(all_grads)


def solution(mesh):
    placed = (
        P(None, "band", None, None),
        P(None, "band", None, None),
        P("section", None, None, None, None),
        P("section", None),
    )
    return jax.shard_map(
        on_device,
        mesh=mesh,
        in_specs=placed,
        out_specs=(P("section", None, "band", None, None), P("section", None, "band", None, None)),
        check_vma=False,
    )
```

```python
import functools

import jax
import jax.numpy as jnp
from jax import lax
from jax.experimental import pallas as pl
from jax.experimental.pallas import tpu as pltpu
from jax.sharding import PartitionSpec as P


DEPTH = 4
BF16 = jnp.bfloat16
F32 = jnp.float32


def spread_columns(ref, base, value, shift, across, channels):
    count = value.shape[0]
    cells = value.reshape(count // across, across, channels)
    before = pltpu.roll(cells, shift % across, 1).reshape(count, channels)
    after = pltpu.roll(cells, -shift % across, 1).reshape(count, channels)
    ref[pl.ds(base, count), 0:channels] = before.astype(BF16)
    ref[pl.ds(base, count), channels : 2 * channels] = value.astype(BF16)
    ref[pl.ds(base, count), 2 * channels : 3 * channels] = after.astype(BF16)


def copy_weights(flags, block, mine, theirs, weights, sems):
    parity, turn, group, place = flags[2], flags[3], flags[4], flags[5]
    rows = mine[0].shape[2]
    back = (group - block + DEPTH) % DEPTH
    slot = jnp.where(back == 2, 3, jnp.where(back == 3, 2, back))
    behind = (0, 1, 3, 2)
    starts = []
    for side, pieces in enumerate((mine, theirs)):
        core = parity if side == 0 else 1 - parity
        for outer in range(DEPTH):
            for inner in range(DEPTH):
                source = pieces[outer] if outer < 3 else pieces[3 + inner // 2]
                index = inner if outer < 3 else inner % 2
                first, second = behind[inner], behind[outer]
                layer = (place - jnp.where(core == 0, first, second) + DEPTH) % DEPTH
                part = core * DEPTH + (turn - jnp.where(core == 0, second, first) + DEPTH) % DEPTH
                starts.append(
                    pltpu.make_async_copy(
                        source.at[index, slot],
                        weights.at[layer, pl.ds(pl.multiple_of(part * rows, 32), rows)],
                        sems.at[layer, part],
                    )
                )
    waits = [
        [
            pltpu.make_async_copy(mine[0].at[0, 0], weights.at[layer, pl.ds(part * rows, rows)], sems.at[layer, part])
            for part in range(2 * DEPTH)
        ]
        for layer in range(DEPTH)
    ]
    for copy in starts:
        copy.start()
    return waits


def forward_kernel(block, flags, own, above, below, *refs):
    mine, theirs = refs[:5], refs[5:10]
    offsets, states, slopes_near, slopes_mid, slopes_far, wide, weights, sems = refs[10:]
    rows, across, channels = own.shape
    is_first = flags[0] == 1
    is_last = flags[1] == 1
    copies = copy_weights(flags, block, mine, theirs, weights, sems)
    step = 2 * across
    for part, piece in enumerate((above, own, below)):
        for pair in range(rows // 2):
            value = piece[2 * pair : 2 * pair + 2].reshape(step, channels).astype(F32)
            spread_columns(wide, (part * rows + 2 * pair) * across, value, 1, across, channels)

    def poles():
        middle = across // 2
        top, bottom = rows * across, (2 * rows - 1) * across

        @pl.when(is_first)
        def _():
            wide[top - across : top - middle, :] = wide[top + middle : top + across, :]
            wide[top - middle : top, :] = wide[top : top + middle, :]

        @pl.when(is_last)
        def _():
            wide[bottom + across : bottom + across + middle, :] = wide[bottom + middle : bottom + across, :]
            wide[bottom + across + middle : bottom + 2 * across, :] = wide[bottom : bottom + middle, :]

    for layer in range(DEPTH):
        poles()
        for copy in copies[layer]:
            copy.wait()
        reach = DEPTH - 1 - layer
        offset = offsets[layer : layer + 1, :]
        first, last = rows - reach, 2 * rows + reach
        carry = []
        for row in range(first, last, 2):
            base = row * across
            preact = None
            for tap in range(3):
                term = jnp.dot(
                    wide[base + (tap - 1) * across : base + (tap - 1) * across + step, :],
                    weights[layer, tap * 3 * channels : (tap + 1) * 3 * channels, :],
                    preferred_element_type=F32,
                )
                preact = term if preact is None else preact + term
            preact = preact + offset
            sigmoid = 0.5 * jnp.tanh(0.5 * preact) + 0.5
            silu = preact * sigmoid
            slope = (sigmoid * (1.0 + preact * (1.0 - sigmoid))).astype(BF16)
            current = wide[base : base + step, channels : 2 * channels].astype(F32)
            result = (current + silu).astype(BF16)
            carry.append((row, result))
            for index in range(2):
                at = row + index
                line = slope[index * across : (index + 1) * across]
                if layer == 0 and rows - 1 <= at < 2 * rows + 1:
                    slopes_near[at - (rows - 1)] = line
                if layer == 1 and rows - 2 <= at < 2 * rows + 2:
                    slopes_mid[at - (rows - 2)] = line
                if layer >= 2 and rows <= at < 2 * rows:
                    slopes_far[layer - 2, at - rows] = line
                if rows <= at < 2 * rows:
                    states[layer, at - rows] = result[index * across : (index + 1) * across]
            if layer < DEPTH - 1 and len(carry) > 1:
                at, value = carry[-2]
                spread_columns(wide, at * across, value.astype(F32), 1, across, channels)
        if layer < DEPTH - 1:
            at, value = carry[-1]
            spread_columns(wide, at * across, value.astype(F32), 1, across, channels)


def backward_kernel(block, flags, own, above, below, slopes_near, slopes_mid, slopes_far, slopes_above, slopes_below, *refs):
    mine, theirs = refs[:5], refs[5:10]
    grads, upstream, wide, poles, weights, sems = refs[10:]
    rows, across, channels = own.shape
    is_first = flags[0] == 1
    is_last = flags[1] == 1
    copies = copy_weights(flags, block, mine, theirs, weights, sems)
    step = 2 * across
    for part, piece in enumerate((above, own, below)):
        upstream[part * rows : (part + 1) * rows] = piece[...]
    poles[...] = jnp.zeros(poles.shape, F32)
    contract = (((1,), (1,)), ((), ()))

    def slope_at(layer, row):
        if layer == 0:
            return slopes_near[row - (rows - 1)]
        if layer == 1:
            return slopes_mid[row - (rows - 2)]
        part, index = divmod(row, rows)
        return (slopes_above, slopes_far, slopes_below)[part][layer - 2, index]

    def tap_weight(layer, tap, column):
        at = (tap * 3 + column) * channels
        return weights[layer, at : at + channels, :]

    for layer in reversed(range(DEPTH)):
        reach = layer + 1
        for row in range(rows - reach, 2 * rows + reach):
            delta = upstream[row].astype(F32) * slope_at(layer, row).astype(F32)
            delta = delta.astype(BF16).astype(F32)
            spread_columns(wide, row * across, delta, -1, across, channels)
        top, bottom, middle = rows * across, (2 * rows - 1) * across, across // 2
        for copy in copies[layer]:
            copy.wait()

        def edge_terms(slot, base, tap):
            for piece in range(2):
                start = base + (1 - piece) * middle
                total = None
                for column in range(3):
                    term = lax.dot_general(
                        wide[start : start + middle, column * channels : (column + 1) * channels],
                        tap_weight(layer, tap, column), contract, preferred_element_type=F32,
                    )
                    total = term if total is None else total + term
                poles[slot, piece * middle : (piece + 1) * middle, :] = total

        @pl.when(is_first)
        def _():
            wide[top - across : top, :] = jnp.zeros((across, 3 * channels), BF16)
            edge_terms(0, top, 0)

        @pl.when(is_last)
        def _():
            wide[bottom + across : bottom + 2 * across, :] = jnp.zeros((across, 3 * channels), BF16)
            edge_terms(1, bottom, 2)

        for row in range(rows - layer, 2 * rows + layer, 2):
            base = row * across
            total = upstream[row : row + 2].reshape(step, channels).astype(F32)
            for tap in range(3):
                for column in range(3):
                    start = base + (1 - tap) * across
                    total = total + lax.dot_general(
                        wide[start : start + step, column * channels : (column + 1) * channels],
                        tap_weight(layer, tap, column), contract, preferred_element_type=F32,
                    )
            for index in range(2):
                at = row + index
                line = total[index * across : (index + 1) * across]
                if at == rows:
                    line = line + poles[0]
                if at == 2 * rows - 1:
                    line = line + poles[1]
                line = line.astype(BF16)
                upstream[at] = line
                if rows <= at < 2 * rows:
                    grads[layer, at - rows] = line


def shift(block, axis, pairs):
    return lax.ppermute(block, axis, pairs)


def on_device(fields, cotangent, kernels, biases):
    band_count = lax.axis_size("band")
    section_count = lax.axis_size("section")
    micro_count, rows, across, channels = fields.shape
    groups = section_count // DEPTH
    band = lax.axis_index("band")
    section = lax.axis_index("section")
    group = section // DEPTH
    place = section % DEPTH
    parity = band % 2
    turn = band // 2 % DEPTH
    flags = jnp.stack([band == 0, band == band_count - 1, parity, turn, group, place]).astype(jnp.int32)
    offsets = lax.all_gather(biases[0], "section").reshape(groups, DEPTH, channels)

    def route(move):
        pairs = []
        for b in range(band_count):
            for s in range(section_count):
                low, y, core, z, x = b // (2 * DEPTH), b // 2 % DEPTH, b % 2, s // DEPTH, s % DEPTH
                y, core, z, x = move(y, core, z, x)
                to = (low * 2 * DEPTH + y % DEPTH * 2 + core) * section_count + z % DEPTH * DEPTH + x % DEPTH
                pairs.append((b * section_count + s, to))
        return pairs

    def carry(block, pairs):
        return lax.ppermute(block, ("band", "section"), pairs)

    def around(block, forth, back):
        middle = block.shape[0] // 2
        behind, ahead = carry(block, route(forth)), carry(block, route(back))
        return behind, ahead, carry(behind[:middle], route(forth)), carry(ahead[middle:], route(back))

    def joined(block, forth, back):
        behind, ahead, low, high = around(block, forth, back)
        return jnp.stack([block, behind, ahead, jnp.concatenate([low, high])])

    quarter = 9 * channels // 2 // DEPTH
    start = (parity * DEPTH + turn) * quarter
    piece = lax.dynamic_slice_in_dim(kernels.reshape(9 * channels, channels), start, quarter, 0)
    piece = joined(piece, lambda y, c, z, x: (y, c, z + 1, x), lambda y, c, z, x: (y, c, z - 1, x))
    piece = joined(
        piece,
        lambda y, c, z, x: (y + c, c, z, x + 1 - c),
        lambda y, c, z, x: (y - c, c, z, x - 1 + c),
    )
    ring = around(
        piece,
        lambda y, c, z, x: (y + 1 - c, c, z, x + c),
        lambda y, c, z, x: (y - 1 + c, c, z, x - c),
    )
    mine = (piece,) + ring
    theirs = tuple(carry(block, route(lambda y, c, z, x: (y, 1 - c, z, x))) for block in mine)

    down = [(i, i + 1) for i in range(band_count - 1)]
    up = [(i + 1, i) for i in range(band_count - 1)]

    def edges(block):
        return shift(block, "band", down), shift(block, "band", up)

    row_shape = (rows, across, channels)
    smem = pl.BlockSpec(memory_space=pltpu.SMEM)
    vmem = pl.BlockSpec(memory_space=pltpu.VMEM)
    hbm = pl.BlockSpec(memory_space=pl.ANY)
    wide = pltpu.VMEM((3 * rows * across, 3 * channels), BF16)
    weight_room = pltpu.VMEM((DEPTH, 9 * channels, channels), BF16)
    sems = pltpu.SemaphoreType.DMA((DEPTH, 2 * DEPTH))
    params = pltpu.CompilerParams(vmem_limit_bytes=48 * 1024 * 1024)

    def shaped(*shape):
        return jax.ShapeDtypeStruct(shape, BF16)

    current = lax.dynamic_index_in_dim(fields, place, 0, keepdims=False)
    all_states, slopes = [], []
    for g in range(groups):
        above, below = edges(current)
        states, near, mid, far = pl.pallas_call(
            functools.partial(forward_kernel, g),
            out_shape=(
                shaped(DEPTH, *row_shape),
                shaped(rows + 2, across, channels),
                shaped(rows + 4, across, channels),
                shaped(2, *row_shape),
            ),
            in_specs=[smem, vmem, vmem, vmem] + [hbm] * 10 + [vmem],
            out_specs=(vmem, vmem, vmem, vmem),
            scratch_shapes=[wide, weight_room, sems],
            compiler_params=params,
            name="forward",
        )(flags, current, above, below, *mine, *theirs, offsets[g])
        current = states[DEPTH - 1]
        all_states.append(states)
        slopes.append((near, mid, far) + edges(far))

    upstream = lax.dynamic_index_in_dim(cotangent, place, 0, keepdims=False)
    all_grads = [None] * groups
    for g in reversed(range(groups)):
        above, below = edges(upstream)
        grads = pl.pallas_call(
            functools.partial(backward_kernel, g),
            out_shape=shaped(DEPTH, *row_shape),
            in_specs=[smem] + [vmem] * 8 + [hbm] * 10,
            out_specs=vmem,
            scratch_shapes=[
                pltpu.VMEM((3 * rows, across, channels), BF16),
                wide,
                pltpu.VMEM((2, across, channels), F32),
                weight_room,
                sems,
            ],
            compiler_params=params,
            name="backward",
        )(flags, upstream, above, below, *slopes[g], *mine, *theirs)
        upstream = grads[0]
        all_grads[g] = grads

    def deliver(blocks):
        kept = lax.select_n(group, *blocks)
        out = jnp.zeros((micro_count,) + row_shape, BF16)
        out = lax.dynamic_update_index_in_dim(out, lax.dynamic_index_in_dim(kept, place, 0, keepdims=False), place, 0)
        for step in range(1, DEPTH):
            send = lax.dynamic_index_in_dim(kept, (place + step) % DEPTH, 0, keepdims=False)
            pairs = [(g * DEPTH + p, g * DEPTH + (p + step) % DEPTH) for g in range(groups) for p in range(DEPTH)]
            received = shift(send, "section", pairs)
            out = lax.dynamic_update_index_in_dim(out, received, (place - step) % DEPTH, 0)
        return out[None]

    return deliver(all_states), deliver(all_grads)


def solution(mesh):
    placed = (
        P(None, "band", None, None),
        P(None, "band", None, None),
        P("section", None, None, None, None),
        P("section", None),
    )
    return jax.shard_map(
        on_device,
        mesh=mesh,
        in_specs=placed,
        out_specs=(P("section", None, "band", None, None), P("section", None, "band", None, None)),
        check_vma=False,
    )
```

```python
import jax
import jax.numpy as jnp
from jax import lax
from jax.experimental import pallas as pl
from jax.experimental.pallas import tpu as pltpu
from jax.sharding import PartitionSpec as P


DEPTH = 4
UNROLL = True
EXTRA = 16
SLOPE_BASE = (0, 10, 18, 24)
SLOPE_ROWS = 28
VMEM_LIMIT = 52 * 1024 * 1024
BF16 = jnp.bfloat16
F32 = jnp.float32


def spread_columns(ref, base, value, shift, across, channels):
    count = value.shape[0]
    cells = value.reshape(count // across, across, channels)
    before = pltpu.roll(cells, shift % across, 1).reshape(count, channels)
    after = pltpu.roll(cells, -shift % across, 1).reshape(count, channels)
    ref[pl.ds(base, count), 0:channels] = before.astype(BF16)
    ref[pl.ds(base, count), channels : 2 * channels] = value.astype(BF16)
    ref[pl.ds(base, count), 2 * channels : 3 * channels] = after.astype(BF16)


def copy_weights(flags, mine, theirs, weights, bias, sems, bias_sems):
    parity, turn, place = flags[2], flags[3], flags[4]
    rows = weights.shape[1] // (2 * DEPTH)
    slot = flags[5]
    behind = (0, 1, 3, 2)
    for side, pieces in enumerate((mine, theirs)):
        core = parity if side == 0 else 1 - parity
        for outer in range(DEPTH):
            for inner in range(DEPTH):
                source = pieces[outer] if outer < 3 else pieces[3 + inner // 2]
                index = inner if outer < 3 else inner % 2
                first, second = behind[inner], behind[outer]
                layer = (place - jnp.where(core == 0, first, second) + DEPTH) % DEPTH
                part = (turn - jnp.where(core == 0, second, first) + DEPTH) % DEPTH
                at = core * DEPTH + part
                pltpu.make_async_copy(
                    source.at[index, slot, pl.ds(0, rows)],
                    weights.at[layer, pl.ds(pl.multiple_of(at * rows, 32), rows)],
                    sems.at[layer, at],
                ).start()
                if side == 0 and bias is not None:
                    pltpu.make_async_copy(
                        source.at[index, slot, pl.ds(rows, EXTRA)], bias.at[layer, part], bias_sems.at[layer, part]
                    ).start()

    def wait(layer):
        for at in range(2 * DEPTH):
            pltpu.make_async_copy(
                mine[0].at[0, 0, pl.ds(0, rows)], weights.at[layer, pl.ds(at * rows, rows)], sems.at[layer, at]
            ).wait()
        if bias is not None:
            for part in range(DEPTH):
                pltpu.make_async_copy(
                    mine[0].at[0, 0, pl.ds(rows, EXTRA)], bias.at[layer, part], bias_sems.at[layer, part]
                ).wait()

    return wait


def forward_kernel(flags, own, above, below, *refs):
    mine, theirs = refs[:5], refs[5:10]
    current, far, all_slopes, kept_states = refs[12:16]
    slopes, states, wide, other, weights, bias, sems, bias_sems, out_sems = refs[16:]
    block, group = flags[6], flags[7]
    save = pltpu.make_async_copy(slopes, all_slopes.at[block], out_sems.at[0])
    keep = pltpu.make_async_copy(states, kept_states, out_sems.at[1])
    rows, across, channels = own.shape
    step = 2 * across
    wait = copy_weights(flags, mine, theirs, weights, bias, sems, bias_sems)
    for part, piece in enumerate((above, own, below)):

        @pl.loop(0, rows)
        def _(row, part=part, piece=piece):
            base = pl.multiple_of((part * rows + row) * across, across)
            spread_columns(wide, base, piece[row].astype(F32), 1, across, channels)

    def poles(ref):
        middle = across // 2
        top, bottom = rows * across, (2 * rows - 1) * across

        @pl.when(flags[0] == 1)
        def _():
            ref[top - across : top - middle, :] = ref[top + middle : top + across, :]
            ref[top - middle : top, :] = ref[top : top + middle, :]

        @pl.when(flags[1] == 1)
        def _():
            ref[bottom + across : bottom + across + middle, :] = ref[bottom + middle : bottom + across, :]
            ref[bottom + across + middle : bottom + 2 * across, :] = ref[bottom : bottom + middle, :]

    for layer in range(DEPTH):
        source, target = (wide, other) if layer % 2 == 0 else (other, wide)
        poles(source)
        wait(layer)
        reach = DEPTH - 1 - layer
        parts = bias[layer, 0].astype(F32)
        offset = (parts[0:1] + parts[1:2]) + parts[2:3]

        @pl.loop(0, rows // 2 + reach, unroll=UNROLL)
        def _(pair, layer=layer, source=source, target=target, reach=reach, offset=offset):
            row = rows - reach + 2 * pair
            base = pl.multiple_of(row * across, across)
            preact = None
            for tap in range(3):
                term = jnp.dot(
                    source[pl.ds(base + (tap - 1) * across, step), :],
                    weights[layer, tap * 3 * channels : (tap + 1) * 3 * channels, :],
                    preferred_element_type=F32,
                )
                preact = term if preact is None else preact + term
            preact = preact + offset
            sigmoid = 0.5 * jnp.tanh(0.5 * preact) + 0.5
            silu = preact * sigmoid
            slope = (sigmoid + silu * (1.0 - sigmoid)).astype(BF16).reshape(2, across, channels)
            before = source[pl.ds(base, step), channels : 2 * channels].astype(F32)
            result = (before + silu).astype(BF16)
            if layer < DEPTH - 1:
                spread_columns(target, base, result.astype(F32), 1, across, channels)
            slopes[pl.ds(SLOPE_BASE[layer] + 2 * pair, 2)] = slope
            if layer == DEPTH - 1:
                current[pl.ds(2 * pair, 2)] = result.reshape(2, across, channels)

        if layer < DEPTH - 1:
            own_cells = target[rows * across : 2 * rows * across, channels : 2 * channels]
            states[layer] = own_cells.reshape(rows, across, channels)
    states[DEPTH - 1] = current[...]
    far[0:rows] = slopes[SLOPE_BASE[3] : SLOPE_BASE[3] + rows]
    far[rows : rows + 2] = slopes[SLOPE_BASE[2] + 2 : SLOPE_BASE[2] + 4]
    save.start()

    @pl.when(block == group)
    def _():
        keep.start()
        keep.wait()

    save.wait()


def backward_kernel(flags, own, above, below, all_slopes, all_above, all_below, *refs):
    mine, theirs = refs[:5], refs[5:10]
    current, kept_grads = refs[11:13]
    grads, slopes, far_above, far_below, upstream, wide, added, weights, sems, out_sems = refs[13:]
    block, group = flags[6], flags[7]
    loads = [
        pltpu.make_async_copy(source.at[block], target, out_sems.at[index])
        for index, (source, target) in enumerate(
            ((all_slopes, slopes), (all_above, far_above), (all_below, far_below))
        )
    ]
    for load in loads:
        load.start()
    keep = pltpu.make_async_copy(grads, kept_grads, out_sems.at[3])
    rows, across, channels = own.shape
    step, middle = 2 * across, across // 2
    wait = copy_weights(flags, mine, theirs, weights, None, sems, None)
    for part, piece in enumerate((above, own, below)):
        for row in range(rows):
            at = (part * rows + row) * across
            upstream[at : at + across] = piece[row]
    added[...] = jnp.zeros(added.shape, F32)
    for load in loads:
        load.wait()
    contract = (((1,), (1,)), ((), ()))

    def tap_weight(layer, tap, column):
        at = (tap * 3 + column) * channels
        return weights[layer, at : at + channels, :]

    for layer in reversed(range(DEPTH)):

        def deltas(first, count, slope_ref, slope_base, layer=layer):
            @pl.loop(0, count)
            def _(index):
                base = pl.multiple_of((first + index) * across, across)
                delta = upstream[pl.ds(base, across)].astype(F32) * slope_ref[slope_base + index].astype(F32)
                spread_columns(wide, base, delta.astype(BF16).astype(F32), -1, across, channels)

        if layer == 3:
            deltas(0, rows, far_above, 0)
            deltas(rows, rows, slopes, SLOPE_BASE[3])
            deltas(2 * rows, rows, far_below, 0)
        elif layer == 2:
            deltas(1, 2, far_above, rows)
            deltas(rows - 1, rows + 2, slopes, SLOPE_BASE[2])
            deltas(2 * rows + 1, 2, far_below, rows)
        else:
            deltas(rows - 1 - layer, rows + 2 + 2 * layer, slopes, SLOPE_BASE[layer] + (2 if layer == 0 else 0))
        top, bottom = rows * across, (2 * rows - 1) * across
        wait(layer)

        def edge_terms(base, tap, layer=layer):
            for piece in range(2):
                start = base + (1 - piece) * middle
                total = None
                for column in range(3):
                    term = lax.dot_general(
                        wide[start : start + middle, column * channels : (column + 1) * channels],
                        tap_weight(layer, tap, column), contract, preferred_element_type=F32,
                    )
                    total = term if total is None else total + term
                added[base + piece * middle : base + (piece + 1) * middle, :] = total

        @pl.when(flags[0] == 1)
        def _():
            wide[top - across : top, :] = jnp.zeros((across, 3 * channels), BF16)
            edge_terms(top, 0)

        @pl.when(flags[1] == 1)
        def _():
            wide[bottom + across : bottom + 2 * across, :] = jnp.zeros((across, 3 * channels), BF16)
            edge_terms(bottom, 2)

        @pl.loop(0, rows // 2 + layer, unroll=UNROLL)
        def _(pair, layer=layer):
            row = rows - layer + 2 * pair
            base = pl.multiple_of(row * across, across)
            total = upstream[pl.ds(base, step)].astype(F32) + added[pl.ds(base, step)]
            for tap in range(3):
                for column in range(3):
                    total = total + lax.dot_general(
                        wide[pl.ds(base + (1 - tap) * across, step), column * channels : (column + 1) * channels],
                        tap_weight(layer, tap, column), contract, preferred_element_type=F32,
                    )
            upstream[pl.ds(base, step)] = total.astype(BF16)

        grads[layer] = upstream[rows * across : 2 * rows * across].reshape(rows, across, channels)
    current[...] = grads[0]

    @pl.when(block == group)
    def _():
        keep.start()
        keep.wait()


def shift(block, axis, pairs):
    return lax.ppermute(block, axis, pairs)


def on_device(fields, cotangent, kernels, biases):
    band_count = lax.axis_size("band")
    section_count = lax.axis_size("section")
    micro_count, rows, across, channels = fields.shape
    groups = section_count // DEPTH
    band = lax.axis_index("band")
    section = lax.axis_index("section")
    group = section // DEPTH
    place = section % DEPTH
    parity = band % 2
    turn = band // 2 % DEPTH
    bias = biases[0]
    high = lax.reduce_precision(bias, 8, 7)
    middle = lax.reduce_precision(bias - high, 8, 7)
    low = bias - high - middle
    extra = jnp.stack([high, middle, low] + [jnp.zeros_like(bias)] * (EXTRA - 3)).astype(BF16)

    def route(move):
        pairs = []
        for b in range(band_count):
            for s in range(section_count):
                low, y, core, z, x = b // (2 * DEPTH), b // 2 % DEPTH, b % 2, s // DEPTH, s % DEPTH
                y, core, z, x = move(y, core, z, x)
                to = (low * 2 * DEPTH + y % DEPTH * 2 + core) * section_count + z % DEPTH * DEPTH + x % DEPTH
                pairs.append((b * section_count + s, to))
        return pairs

    def carry(block, pairs):
        return lax.ppermute(block, ("band", "section"), pairs)

    def around(block, forth, back):
        middle = block.shape[0] // 2
        behind, ahead = carry(block, route(forth)), carry(block, route(back))
        return behind, ahead, carry(behind[:middle], route(forth)), carry(ahead[middle:], route(back))

    def joined(block, forth, back):
        behind, ahead, low, high = around(block, forth, back)
        return jnp.stack([block, behind, ahead, jnp.concatenate([low, high])])

    quarter = 9 * channels // 2 // DEPTH
    start = (parity * DEPTH + turn) * quarter
    piece = lax.dynamic_slice_in_dim(kernels.reshape(9 * channels, channels), start, quarter, 0)
    piece = jnp.concatenate([piece, extra])
    piece = joined(piece, lambda y, c, z, x: (y, c, z + 1, x), lambda y, c, z, x: (y, c, z - 1, x))
    piece = joined(
        piece,
        lambda y, c, z, x: (y + c, c, z, x + 1 - c),
        lambda y, c, z, x: (y - c, c, z, x - 1 + c),
    )
    ring = around(
        piece,
        lambda y, c, z, x: (y + 1 - c, c, z, x + c),
        lambda y, c, z, x: (y - 1 + c, c, z, x - c),
    )
    mine = (piece,) + ring
    theirs = tuple(carry(block, route(lambda y, c, z, x: (y, 1 - c, z, x))) for block in mine)

    down = [(i, i + 1) for i in range(band_count - 1)]
    up = [(i + 1, i) for i in range(band_count - 1)]

    def edges(block):
        return shift(block, "band", down), shift(block, "band", up)

    row_shape = (rows, across, channels)
    smem = pl.BlockSpec(memory_space=pltpu.SMEM)
    vmem = pl.BlockSpec(memory_space=pltpu.VMEM)
    hbm = pl.BlockSpec(memory_space=pl.ANY)
    wide = pltpu.VMEM((3 * rows * across, 3 * channels), BF16)
    weight_room = pltpu.VMEM((DEPTH, 9 * channels, channels), BF16)
    bias_room = pltpu.VMEM((DEPTH, DEPTH, EXTRA, channels), BF16)
    sems = pltpu.SemaphoreType.DMA((DEPTH, 2 * DEPTH))
    bias_sems = pltpu.SemaphoreType.DMA((DEPTH, DEPTH))
    params = pltpu.CompilerParams(vmem_limit_bytes=VMEM_LIMIT)

    def shaped(*shape):
        return jax.ShapeDtypeStruct(shape, BF16)

    both = jnp.stack([lax.dynamic_index_in_dim(block, place, 0, keepdims=False) for block in (fields, cotangent)])
    above, below = edges(both)
    current, upstream = both[0], both[1]
    start_edges = (above[1], below[1])
    above, below = above[0], below[0]
    cells = (across, channels)

    def flags_of(block):
        slot = (group - block) % groups
        slot = jnp.where(slot == 2, 3, jnp.where(slot == 3, 2, slot))
        return jnp.stack(
            [band == 0, band == band_count - 1, parity, turn, place, slot, block, group]
        ).astype(jnp.int32)

    forward = pl.pallas_call(
        forward_kernel,
        out_shape=(
            shaped(*row_shape),
            shaped(rows + 2, *cells),
            shaped(groups, SLOPE_ROWS, *cells),
            shaped(DEPTH, *row_shape),
        ),
        in_specs=[smem, vmem, vmem, vmem] + [hbm] * 12,
        out_specs=(vmem, vmem, hbm, hbm),
        input_output_aliases={14: 2, 15: 3},
        scratch_shapes=[
            pltpu.VMEM((SLOPE_ROWS, *cells), BF16),
            pltpu.VMEM((DEPTH, *row_shape), BF16),
            wide,
            wide,
            weight_room,
            bias_room,
            sems,
            bias_sems,
            pltpu.SemaphoreType.DMA((2,)),
        ],
        compiler_params=params,
        name="forward",
    )
    backward = pl.pallas_call(
        backward_kernel,
        out_shape=(shaped(*row_shape), shaped(DEPTH, *row_shape)),
        in_specs=[smem] + [vmem] * 3 + [hbm] * 14,
        out_specs=(vmem, hbm),
        input_output_aliases={17: 1},
        scratch_shapes=[
            pltpu.VMEM((DEPTH, *row_shape), BF16),
            pltpu.VMEM((SLOPE_ROWS, *cells), BF16),
            pltpu.VMEM((rows + 2, *cells), BF16),
            pltpu.VMEM((rows + 2, *cells), BF16),
            pltpu.VMEM((3 * rows * across, channels), BF16),
            wide,
            pltpu.VMEM((3 * rows * across, channels), F32),
            weight_room,
            sems,
            pltpu.SemaphoreType.DMA((4,)),
        ],
        compiler_params=params,
        name="backward",
    )

    def forward_step(block, state):
        current, above, below, far, slopes, states, far_above, far_below = state
        last_above, last_below = edges(far)
        before = (block + groups - 1) % groups
        far_above = lax.dynamic_update_index_in_dim(far_above, last_above, before, 0)
        far_below = lax.dynamic_update_index_in_dim(far_below, last_below, before, 0)
        current, far, slopes, states = forward(
            flags_of(block), current, above, below, *mine, *theirs, slopes, states
        )
        above, below = lax.cond(block < groups - 1, edges, lambda _: (above, below), current)
        return current, above, below, far, slopes, states, far_above, far_below

    far = jnp.zeros((rows + 2, *cells), BF16)
    far_all = jnp.zeros((groups, rows + 2, *cells), BF16)
    state = (
        current, above, below, far, jnp.zeros((groups, SLOPE_ROWS, *cells), BF16),
        jnp.zeros((DEPTH, *row_shape), BF16), far_all, far_all,
    )
    state = lax.fori_loop(0, groups, forward_step, state)
    far, slopes, states, far_above, far_below = state[3:]
    last_above, last_below = edges(far)
    far_above = lax.dynamic_update_index_in_dim(far_above, last_above, groups - 1, 0)
    far_below = lax.dynamic_update_index_in_dim(far_below, last_below, groups - 1, 0)

    def backward_step(step, state):
        upstream, above, below, grads = state
        block = groups - 1 - step
        upstream, grads = backward(
            flags_of(block), upstream, above, below, slopes, far_above, far_below, *mine, *theirs, grads
        )
        above, below = lax.cond(block > 0, edges, lambda _: (above, below), upstream)
        return upstream, above, below, grads

    state = (upstream, *start_edges, jnp.zeros((DEPTH, *row_shape), BF16))
    grads = lax.fori_loop(0, groups, backward_step, state)[3]

    def deliver(kept):
        out = jnp.zeros((micro_count,) + row_shape, BF16)
        out = lax.dynamic_update_index_in_dim(out, lax.dynamic_index_in_dim(kept, place, 0, keepdims=False), place, 0)
        for step in range(1, DEPTH):
            send = lax.dynamic_index_in_dim(kept, (place + step) % DEPTH, 0, keepdims=False)
            pairs = [(g * DEPTH + p, g * DEPTH + (p + step) % DEPTH) for g in range(groups) for p in range(DEPTH)]
            received = shift(send, "section", pairs)
            out = lax.dynamic_update_index_in_dim(out, received, (place - step) % DEPTH, 0)
        return out[None]

    return deliver(states), deliver(grads)


def solution(mesh):
    placed = (
        P(None, "band", None, None),
        P(None, "band", None, None),
        P("section", None, None, None, None),
        P("section", None),
    )
    return jax.shard_map(
        on_device,
        mesh=mesh,
        in_specs=placed,
        out_specs=(P("section", None, "band", None, None), P("section", None, "band", None, None)),
        check_vma=False,
    )
```

```python
import jax
import jax.numpy as jnp
from jax import lax
from jax.experimental import pallas as pl
from jax.experimental.pallas import tpu as pltpu
from jax.sharding import PartitionSpec as P


DEPTH = 4
UNROLL = True
EXTRA = 16
SLOPE_BASE = (0, 10, 18, 24)
SLOPE_ROWS = 28
VMEM_LIMIT = 52 * 1024 * 1024
BF16 = jnp.bfloat16
F32 = jnp.float32


def spread_columns(ref, base, value, shift, across, channels):
    count = value.shape[0]
    cells = value.reshape(count // across, across, channels)
    before = pltpu.roll(cells, shift % across, 1).reshape(count, channels)
    after = pltpu.roll(cells, -shift % across, 1).reshape(count, channels)
    ref[pl.ds(base, count), 0:channels] = before.astype(BF16)
    ref[pl.ds(base, count), channels : 2 * channels] = value.astype(BF16)
    ref[pl.ds(base, count), 2 * channels : 3 * channels] = after.astype(BF16)


def copy_weights(flags, mine, theirs, weights, bias, sems, bias_sems):
    parity, turn, place = flags[2], flags[3], flags[4]
    rows = weights.shape[1] // (2 * DEPTH)
    slot = flags[5]
    behind = (0, 1, 3, 2)
    for side, pieces in enumerate((mine, theirs)):
        core = parity if side == 0 else 1 - parity
        for outer in range(DEPTH):
            for inner in range(DEPTH):
                source = pieces[outer] if outer < 3 else pieces[3 + inner // 2]
                index = inner if outer < 3 else inner % 2
                first, second = behind[inner], behind[outer]
                layer = (place - jnp.where(core == 0, first, second) + DEPTH) % DEPTH
                part = (turn - jnp.where(core == 0, second, first) + DEPTH) % DEPTH
                at = core * DEPTH + part
                pltpu.make_async_copy(
                    source.at[index, slot, pl.ds(0, rows)],
                    weights.at[layer, pl.ds(pl.multiple_of(at * rows, 32), rows)],
                    sems.at[layer, at],
                ).start()
                if side == 0 and bias is not None:
                    pltpu.make_async_copy(
                        source.at[index, slot, pl.ds(rows, EXTRA)], bias.at[layer, part], bias_sems.at[layer, part]
                    ).start()

    def wait(layer):
        for at in range(2 * DEPTH):
            pltpu.make_async_copy(
                mine[0].at[0, 0, pl.ds(0, rows)], weights.at[layer, pl.ds(at * rows, rows)], sems.at[layer, at]
            ).wait()
        if bias is not None:
            for part in range(DEPTH):
                pltpu.make_async_copy(
                    mine[0].at[0, 0, pl.ds(rows, EXTRA)], bias.at[layer, part], bias_sems.at[layer, part]
                ).wait()

    return wait


def forward_kernel(flags, own, above, below, *refs):
    mine, theirs = refs[:5], refs[5:10]
    edge, all_slopes, kept_states, all_above, all_below = refs[14:19]
    slopes, states, wide, other, weights, bias, sems, bias_sems, out_sems = refs[19:]
    block, group = flags[6], flags[7]
    save = pltpu.make_async_copy(slopes, all_slopes.at[block], out_sems.at[0])
    keep = pltpu.make_async_copy(states, kept_states, out_sems.at[1])
    rows, across, channels = states.shape[1:]
    step = 2 * across
    wait = copy_weights(flags, mine, theirs, weights, bias, sems, bias_sems)
    last_block = (block + DEPTH - 1) % DEPTH
    pass_on = [
        pltpu.make_async_copy(piece.at[pl.ds(rows, rows + 2)], kept.at[last_block], out_sems.at[2 + index])
        for index, (piece, kept) in enumerate(((above, all_above), (below, all_below)))
    ]
    for copy in pass_on:
        copy.start()
    for part, piece in enumerate((above, own, below)):

        @pl.loop(0, rows)
        def _(row, part=part, piece=piece):
            base = pl.multiple_of((part * rows + row) * across, across)
            spread_columns(wide, base, piece[row].astype(F32), 1, across, channels)

    def poles(ref):
        middle = across // 2
        top, bottom = rows * across, (2 * rows - 1) * across

        @pl.when(flags[0] == 1)
        def _():
            ref[top - across : top - middle, :] = ref[top + middle : top + across, :]
            ref[top - middle : top, :] = ref[top : top + middle, :]

        @pl.when(flags[1] == 1)
        def _():
            ref[bottom + across : bottom + across + middle, :] = ref[bottom + middle : bottom + across, :]
            ref[bottom + across + middle : bottom + 2 * across, :] = ref[bottom : bottom + middle, :]

    for layer in range(DEPTH):
        source, target = (wide, other) if layer % 2 == 0 else (other, wide)
        poles(source)
        wait(layer)
        reach = DEPTH - 1 - layer
        parts = bias[layer, 0].astype(F32)
        offset = (parts[0:1] + parts[1:2]) + parts[2:3]

        @pl.loop(0, rows // 2 + reach, unroll=UNROLL)
        def _(pair, layer=layer, source=source, target=target, reach=reach, offset=offset):
            row = rows - reach + 2 * pair
            base = pl.multiple_of(row * across, across)
            preact = None
            for tap in range(3):
                term = jnp.dot(
                    source[pl.ds(base + (tap - 1) * across, step), :],
                    weights[layer, tap * 3 * channels : (tap + 1) * 3 * channels, :],
                    preferred_element_type=F32,
                )
                preact = term if preact is None else preact + term
            preact = preact + offset
            sigmoid = 0.5 * jnp.tanh(0.5 * preact) + 0.5
            silu = preact * sigmoid
            slope = (sigmoid + silu * (1.0 - sigmoid)).astype(BF16).reshape(2, across, channels)
            before = source[pl.ds(base, step), channels : 2 * channels].astype(F32)
            result = (before + silu).astype(BF16)
            if layer < DEPTH - 1:
                spread_columns(target, base, result.astype(F32), 1, across, channels)
            slopes[pl.ds(SLOPE_BASE[layer] + 2 * pair, 2)] = slope
            if layer == DEPTH - 1:
                edge[pl.ds(2 * pair, 2)] = result.reshape(2, across, channels)

        if layer < DEPTH - 1:
            own_cells = target[rows * across : 2 * rows * across, channels : 2 * channels]
            states[layer] = own_cells.reshape(rows, across, channels)
    states[DEPTH - 1] = edge[0:rows]
    edge[rows : 2 * rows] = slopes[SLOPE_BASE[3] : SLOPE_BASE[3] + rows]
    edge[2 * rows :] = slopes[SLOPE_BASE[2] + 2 : SLOPE_BASE[2] + 4]
    save.start()

    @pl.when(block == group)
    def _():
        keep.start()
        keep.wait()

    for copy in [save] + pass_on:
        copy.wait()


def backward_kernel(flags, own, above, below, all_slopes, all_above, all_below, *refs):
    mine, theirs = refs[:5], refs[5:10]
    current, kept_grads = refs[11:13]
    grads, slopes, far_above, far_below, upstream, wide, added, weights, sems, out_sems = refs[13:]
    block, group = flags[6], flags[7]
    loads = [
        pltpu.make_async_copy(source.at[block], target, out_sems.at[index])
        for index, (source, target) in enumerate(
            ((all_slopes, slopes), (all_above, far_above), (all_below, far_below))
        )
    ]
    for load in loads:
        load.start()
    keep = pltpu.make_async_copy(grads, kept_grads, out_sems.at[3])
    rows, across, channels = own.shape
    step, middle = 2 * across, across // 2
    wait = copy_weights(flags, mine, theirs, weights, None, sems, None)
    for part, piece in enumerate((above, own, below)):
        for row in range(rows):
            at = (part * rows + row) * across
            upstream[at : at + across] = piece[row]
    added[...] = jnp.zeros(added.shape, F32)
    for load in loads:
        load.wait()
    contract = (((1,), (1,)), ((), ()))

    def tap_weight(layer, tap, column):
        at = (tap * 3 + column) * channels
        return weights[layer, at : at + channels, :]

    for layer in reversed(range(DEPTH)):

        def deltas(first, count, slope_ref, slope_base, layer=layer):
            @pl.loop(0, count)
            def _(index):
                base = pl.multiple_of((first + index) * across, across)
                delta = upstream[pl.ds(base, across)].astype(F32) * slope_ref[slope_base + index].astype(F32)
                spread_columns(wide, base, delta.astype(BF16).astype(F32), -1, across, channels)

        if layer == 3:
            deltas(0, rows, far_above, 0)
            deltas(rows, rows, slopes, SLOPE_BASE[3])
            deltas(2 * rows, rows, far_below, 0)
        elif layer == 2:
            deltas(1, 2, far_above, rows)
            deltas(rows - 1, rows + 2, slopes, SLOPE_BASE[2])
            deltas(2 * rows + 1, 2, far_below, rows)
        else:
            deltas(rows - 1 - layer, rows + 2 + 2 * layer, slopes, SLOPE_BASE[layer] + (2 if layer == 0 else 0))
        top, bottom = rows * across, (2 * rows - 1) * across
        wait(layer)

        def edge_terms(base, tap, layer=layer):
            for piece in range(2):
                start = base + (1 - piece) * middle
                total = None
                for column in range(3):
                    term = lax.dot_general(
                        wide[start : start + middle, column * channels : (column + 1) * channels],
                        tap_weight(layer, tap, column), contract, preferred_element_type=F32,
                    )
                    total = term if total is None else total + term
                added[base + piece * middle : base + (piece + 1) * middle, :] = total

        @pl.when(flags[0] == 1)
        def _():
            wide[top - across : top, :] = jnp.zeros((across, 3 * channels), BF16)
            edge_terms(top, 0)

        @pl.when(flags[1] == 1)
        def _():
            wide[bottom + across : bottom + 2 * across, :] = jnp.zeros((across, 3 * channels), BF16)
            edge_terms(bottom, 2)

        @pl.loop(0, rows // 2 + layer, unroll=UNROLL)
        def _(pair, layer=layer):
            row = rows - layer + 2 * pair
            base = pl.multiple_of(row * across, across)
            total = upstream[pl.ds(base, step)].astype(F32) + added[pl.ds(base, step)]
            for tap in range(3):
                for column in range(3):
                    total = total + lax.dot_general(
                        wide[pl.ds(base + (1 - tap) * across, step), column * channels : (column + 1) * channels],
                        tap_weight(layer, tap, column), contract, preferred_element_type=F32,
                    )
            upstream[pl.ds(base, step)] = total.astype(BF16)

        grads[layer] = upstream[rows * across : 2 * rows * across].reshape(rows, across, channels)
    current[...] = grads[0]

    @pl.when(block == group)
    def _():
        keep.start()
        keep.wait()


def shift(block, axis, pairs):
    return lax.ppermute(block, axis, pairs)


def on_device(fields, cotangent, kernels, biases):
    band_count = lax.axis_size("band")
    section_count = lax.axis_size("section")
    micro_count, rows, across, channels = fields.shape
    groups = section_count // DEPTH
    band = lax.axis_index("band")
    section = lax.axis_index("section")
    group = section // DEPTH
    place = section % DEPTH
    parity = band % 2
    turn = band // 2 % DEPTH
    bias = biases[0]
    high = lax.reduce_precision(bias, 8, 7)
    middle = lax.reduce_precision(bias - high, 8, 7)
    low = bias - high - middle
    extra = jnp.stack([high, middle, low] + [jnp.zeros_like(bias)] * (EXTRA - 3)).astype(BF16)

    def route(move):
        pairs = []
        for b in range(band_count):
            for s in range(section_count):
                low, y, core, z, x = b // (2 * DEPTH), b // 2 % DEPTH, b % 2, s // DEPTH, s % DEPTH
                y, core, z, x = move(y, core, z, x)
                to = (low * 2 * DEPTH + y % DEPTH * 2 + core) * section_count + z % DEPTH * DEPTH + x % DEPTH
                pairs.append((b * section_count + s, to))
        return pairs

    def carry(block, pairs):
        return lax.ppermute(block, ("band", "section"), pairs)

    def around(block, forth, back):
        middle = block.shape[0] // 2
        behind, ahead = carry(block, route(forth)), carry(block, route(back))
        return behind, ahead, carry(behind[:middle], route(forth)), carry(ahead[middle:], route(back))

    def joined(block, forth, back):
        behind, ahead, low, high = around(block, forth, back)
        return jnp.stack([block, behind, ahead, jnp.concatenate([low, high])])

    down = [(i, i + 1) for i in range(band_count - 1)]
    up = [(i + 1, i) for i in range(band_count - 1)]

    def edges(block):
        return shift(block, "band", down), shift(block, "band", up)

    current, upstream = (lax.dynamic_index_in_dim(block, place, 0, keepdims=False) for block in (fields, cotangent))
    edge = jnp.concatenate([current, upstream, upstream[:2]])
    edge_above, edge_below = edges(edge)

    quarter = 9 * channels // 2 // DEPTH
    start = (parity * DEPTH + turn) * quarter
    piece = lax.dynamic_slice_in_dim(kernels.reshape(9 * channels, channels), start, quarter, 0)
    piece = jnp.concatenate([piece, extra])
    piece = joined(piece, lambda y, c, z, x: (y, c, z + 1, x), lambda y, c, z, x: (y, c, z - 1, x))
    piece = pl.pallas_call(
        lambda *refs: None,
        out_shape=jax.ShapeDtypeStruct(piece.shape, BF16),
        in_specs=[pl.BlockSpec(memory_space=pl.ANY)] * 3,
        out_specs=pl.BlockSpec(memory_space=pl.ANY),
        input_output_aliases={0: 0},
        name="after",
    )(piece, edge_above, edge_below)
    piece = joined(
        piece,
        lambda y, c, z, x: (y + c, c, z, x + 1 - c),
        lambda y, c, z, x: (y - c, c, z, x - 1 + c),
    )
    ring = around(
        piece,
        lambda y, c, z, x: (y + 1 - c, c, z, x + c),
        lambda y, c, z, x: (y - 1 + c, c, z, x - c),
    )
    mine = (piece,) + ring
    theirs = tuple(carry(block, route(lambda y, c, z, x: (y, 1 - c, z, x))) for block in mine)

    row_shape = (rows, across, channels)
    smem = pl.BlockSpec(memory_space=pltpu.SMEM)
    vmem = pl.BlockSpec(memory_space=pltpu.VMEM)
    hbm = pl.BlockSpec(memory_space=pl.ANY)
    wide = pltpu.VMEM((3 * rows * across, 3 * channels), BF16)
    weight_room = pltpu.VMEM((DEPTH, 9 * channels, channels), BF16)
    bias_room = pltpu.VMEM((DEPTH, DEPTH, EXTRA, channels), BF16)
    sems = pltpu.SemaphoreType.DMA((DEPTH, 2 * DEPTH))
    bias_sems = pltpu.SemaphoreType.DMA((DEPTH, DEPTH))
    params = pltpu.CompilerParams(vmem_limit_bytes=VMEM_LIMIT)

    def shaped(*shape):
        return jax.ShapeDtypeStruct(shape, BF16)

    cells = (across, channels)

    def flags_of(block):
        slot = (group - block) % groups
        slot = jnp.where(slot == 2, 3, jnp.where(slot == 3, 2, slot))
        return jnp.stack(
            [band == 0, band == band_count - 1, parity, turn, place, slot, block, group]
        ).astype(jnp.int32)

    forward = pl.pallas_call(
        forward_kernel,
        out_shape=(
            shaped(2 * rows + 2, *cells),
            shaped(groups, SLOPE_ROWS, *cells),
            shaped(DEPTH, *row_shape),
            shaped(groups, rows + 2, *cells),
            shaped(groups, rows + 2, *cells),
        ),
        in_specs=[smem, vmem, vmem, vmem] + [hbm] * 14,
        out_specs=(vmem,) + (hbm,) * 4,
        input_output_aliases={14: 1, 15: 2, 16: 3, 17: 4},
        scratch_shapes=[
            pltpu.VMEM((SLOPE_ROWS, *cells), BF16),
            pltpu.VMEM((DEPTH, *row_shape), BF16),
            wide,
            wide,
            weight_room,
            bias_room,
            sems,
            bias_sems,
            pltpu.SemaphoreType.DMA((4,)),
        ],
        compiler_params=params,
        name="forward",
    )
    backward = pl.pallas_call(
        backward_kernel,
        out_shape=(shaped(*row_shape), shaped(DEPTH, *row_shape)),
        in_specs=[smem] + [vmem] * 3 + [hbm] * 14,
        out_specs=(vmem, hbm),
        input_output_aliases={17: 1},
        scratch_shapes=[
            pltpu.VMEM((DEPTH, *row_shape), BF16),
            pltpu.VMEM((SLOPE_ROWS, *cells), BF16),
            pltpu.VMEM((rows + 2, *cells), BF16),
            pltpu.VMEM((rows + 2, *cells), BF16),
            pltpu.VMEM((3 * rows * across, channels), BF16),
            wide,
            pltpu.VMEM((3 * rows * across, channels), F32),
            weight_room,
            sems,
            pltpu.SemaphoreType.DMA((4,)),
        ],
        compiler_params=params,
        name="backward",
    )

    def forward_step(block, state):
        edge, above, below, *kept = state
        edge, *kept = forward(flags_of(block), edge, above, below, *mine, *theirs, *kept)
        return edge, *edges(edge), *kept

    room = pl.pallas_call(
        lambda *refs: None,
        out_shape=(
            shaped(groups, SLOPE_ROWS, *cells),
            shaped(DEPTH, *row_shape),
            shaped(groups, rows + 2, *cells),
            shaped(groups, rows + 2, *cells),
            shaped(DEPTH, *row_shape),
        ),
        out_specs=(hbm,) * 5,
        name="room",
    )()
    state = (edge, edge_above, edge_below, *room[:4])
    edge, above, below, slopes, states, far_above, far_below = lax.fori_loop(0, groups, forward_step, state)
    far_above = lax.dynamic_update_index_in_dim(far_above, above[rows:], groups - 1, 0)
    far_below = lax.dynamic_update_index_in_dim(far_below, below[rows:], groups - 1, 0)

    def backward_step(step, state):
        upstream, above, below, grads = state
        block = groups - 1 - step
        upstream, grads = backward(
            flags_of(block), upstream, above, below, slopes, far_above, far_below, *mine, *theirs, grads
        )
        above, below = lax.cond(block > 0, edges, lambda _: (above, below), upstream)
        return upstream, above, below, grads

    state = (upstream, edge_above[rows : 2 * rows], edge_below[rows : 2 * rows], room[4])
    grads = lax.fori_loop(0, groups, backward_step, state)[3]

    def deliver(kept):
        out = jnp.zeros((micro_count,) + row_shape, BF16)
        out = lax.dynamic_update_index_in_dim(out, lax.dynamic_index_in_dim(kept, place, 0, keepdims=False), place, 0)
        for step in range(1, DEPTH):
            send = lax.dynamic_index_in_dim(kept, (place + step) % DEPTH, 0, keepdims=False)
            pairs = [(g * DEPTH + p, g * DEPTH + (p + step) % DEPTH) for g in range(groups) for p in range(DEPTH)]
            received = shift(send, "section", pairs)
            out = lax.dynamic_update_index_in_dim(out, received, (place - step) % DEPTH, 0)
        return out[None]

    return deliver(states), deliver(grads)


def solution(mesh):
    placed = (
        P(None, "band", None, None),
        P(None, "band", None, None),
        P("section", None, None, None, None),
        P("section", None),
    )
    return jax.shard_map(
        on_device,
        mesh=mesh,
        in_specs=placed,
        out_specs=(P("section", None, "band", None, None), P("section", None, "band", None, None)),
        check_vma=False,
    )
```

```python
import jax
import jax.numpy as jnp
from jax import lax
from jax.experimental import pallas as pl
from jax.experimental.pallas import tpu as pltpu
from jax.sharding import PartitionSpec as P


DEPTH = 4
UNROLL = True
EXTRA = 16
SLOPE_BASE = (0, 10, 18, 24)
SLOPE_ROWS = 28
VMEM_LIMIT = 52 * 1024 * 1024
BF16 = jnp.bfloat16
F32 = jnp.float32


def spread_columns(ref, base, value, shift, across, channels):
    count = value.shape[0]
    cells = value.reshape(count // across, across, channels)
    before = pltpu.roll(cells, shift % across, 1).reshape(count, channels)
    after = pltpu.roll(cells, -shift % across, 1).reshape(count, channels)
    ref[pl.ds(base, count), 0:channels] = before.astype(BF16)
    ref[pl.ds(base, count), channels : 2 * channels] = value.astype(BF16)
    ref[pl.ds(base, count), 2 * channels : 3 * channels] = after.astype(BF16)


def copy_weights(flags, mine, theirs, weights, bias, sems, bias_sems):
    parity, turn, place = flags[2], flags[3], flags[4]
    rows = weights.shape[1] // (2 * DEPTH)
    slot = flags[5]
    behind = (0, 1, 3, 2)
    for side, pieces in enumerate((mine, theirs)):
        core = parity if side == 0 else 1 - parity
        for outer in range(DEPTH):
            for inner in range(DEPTH):
                source = pieces[outer] if outer < 3 else pieces[3 + inner // 2]
                index = inner if outer < 3 else inner % 2
                first, second = behind[inner], behind[outer]
                layer = (place - jnp.where(core == 0, first, second) + DEPTH) % DEPTH
                part = (turn - jnp.where(core == 0, second, first) + DEPTH) % DEPTH
                at = core * DEPTH + part
                pltpu.make_async_copy(
                    source.at[index, slot, pl.ds(0, rows)],
                    weights.at[layer, pl.ds(pl.multiple_of(at * rows, 32), rows)],
                    sems.at[layer, at],
                ).start()
                if side == 0 and bias is not None:
                    pltpu.make_async_copy(
                        source.at[index, slot, pl.ds(rows, EXTRA)], bias.at[layer, part], bias_sems.at[layer, part]
                    ).start()

    def wait(layer):
        for at in range(2 * DEPTH):
            pltpu.make_async_copy(
                mine[0].at[0, 0, pl.ds(0, rows)], weights.at[layer, pl.ds(at * rows, rows)], sems.at[layer, at]
            ).wait()
        if bias is not None:
            for part in range(DEPTH):
                pltpu.make_async_copy(
                    mine[0].at[0, 0, pl.ds(rows, EXTRA)], bias.at[layer, part], bias_sems.at[layer, part]
                ).wait()

    return wait


def forward_kernel(flags, own, outside, inside, *refs):
    mine, theirs = refs[:5], refs[5:10]
    edge, all_slopes, kept_states, all_outside, all_inside = refs[14:19]
    slopes, states, wide, other, weights, bias, sems, bias_sems, out_sems = refs[19:]
    block, group = flags[6], flags[7]
    save = pltpu.make_async_copy(slopes, all_slopes.at[block], out_sems.at[0])
    keep = pltpu.make_async_copy(states, kept_states, out_sems.at[1])
    rows, across, channels = states.shape[1:]
    step = 2 * across
    wait = copy_weights(flags, mine, theirs, weights, bias, sems, bias_sems)
    last_block = (block + DEPTH - 1) % DEPTH
    pass_on = [
        pltpu.make_async_copy(piece.at[pl.ds(rows, rows + 2)], kept.at[last_block], out_sems.at[2 + index])
        for index, (piece, kept) in enumerate(((outside, all_outside), (inside, all_inside)))
    ]
    for copy in pass_on:
        copy.start()
    odd = flags[2] == 1
    for part in range(3):

        @pl.loop(0, rows)
        def _(row, part=part):
            base = pl.multiple_of((part * rows + row) * across, across)
            if part == 1:
                line = own[row].astype(F32)
            else:
                pair = (inside, outside) if part == 0 else (outside, inside)
                line = jnp.where(odd, pair[0][row].astype(F32), pair[1][row].astype(F32))
            spread_columns(wide, base, line, 1, across, channels)

    def poles(ref):
        middle = across // 2
        top, bottom = rows * across, (2 * rows - 1) * across

        @pl.when(flags[0] == 1)
        def _():
            ref[top - across : top - middle, :] = ref[top + middle : top + across, :]
            ref[top - middle : top, :] = ref[top : top + middle, :]

        @pl.when(flags[1] == 1)
        def _():
            ref[bottom + across : bottom + across + middle, :] = ref[bottom + middle : bottom + across, :]
            ref[bottom + across + middle : bottom + 2 * across, :] = ref[bottom : bottom + middle, :]

    for layer in range(DEPTH):
        source, target = (wide, other) if layer % 2 == 0 else (other, wide)
        poles(source)
        wait(layer)
        reach = DEPTH - 1 - layer
        parts = bias[layer, 0].astype(F32)
        offset = (parts[0:1] + parts[1:2]) + parts[2:3]

        @pl.loop(0, rows // 2 + reach, unroll=UNROLL)
        def _(pair, layer=layer, source=source, target=target, reach=reach, offset=offset):
            row = rows - reach + 2 * pair
            base = pl.multiple_of(row * across, across)
            preact = None
            for tap in range(3):
                term = jnp.dot(
                    source[pl.ds(base + (tap - 1) * across, step), :],
                    weights[layer, tap * 3 * channels : (tap + 1) * 3 * channels, :],
                    preferred_element_type=F32,
                )
                preact = term if preact is None else preact + term
            preact = preact + offset
            sigmoid = 0.5 * jnp.tanh(0.5 * preact) + 0.5
            silu = preact * sigmoid
            slope = (sigmoid + silu * (1.0 - sigmoid)).astype(BF16).reshape(2, across, channels)
            before = source[pl.ds(base, step), channels : 2 * channels].astype(F32)
            result = (before + silu).astype(BF16)
            if layer < DEPTH - 1:
                spread_columns(target, base, result.astype(F32), 1, across, channels)
            slopes[pl.ds(SLOPE_BASE[layer] + 2 * pair, 2)] = slope
            if layer == DEPTH - 1:
                edge[pl.ds(2 * pair, 2)] = result.reshape(2, across, channels)

        if layer < DEPTH - 1:
            own_cells = target[rows * across : 2 * rows * across, channels : 2 * channels]
            states[layer] = own_cells.reshape(rows, across, channels)
    states[DEPTH - 1] = edge[0:rows]
    edge[rows : 2 * rows] = slopes[SLOPE_BASE[3] : SLOPE_BASE[3] + rows]
    edge[2 * rows :] = slopes[SLOPE_BASE[2] + 2 : SLOPE_BASE[2] + 4]
    save.start()

    @pl.when(block == group)
    def _():
        keep.start()
        keep.wait()

    for copy in [save] + pass_on:
        copy.wait()


def backward_kernel(flags, own, outside, inside, all_slopes, all_outside, all_inside, *refs):
    mine, theirs = refs[:5], refs[5:10]
    current, kept_grads = refs[11:13]
    grads, slopes, far_above, far_below, upstream, wide, added, weights, sems, out_sems = refs[13:]
    block, group = flags[6], flags[7]
    odd = flags[2] == 1
    for swapped in range(2):

        @pl.when(flags[2] == swapped)
        def _(swapped=swapped):
            ends = (all_inside, all_outside) if swapped else (all_outside, all_inside)
            for index, (source, target) in enumerate(zip(ends, (far_above, far_below))):
                pltpu.make_async_copy(source.at[block], target, out_sems.at[index]).start()

    pltpu.make_async_copy(all_slopes.at[block], slopes, out_sems.at[2]).start()
    loads = [
        pltpu.make_async_copy(source.at[block], target, out_sems.at[index])
        for index, (source, target) in enumerate(
            ((all_outside, far_above), (all_inside, far_below), (all_slopes, slopes))
        )
    ]
    keep = pltpu.make_async_copy(grads, kept_grads, out_sems.at[3])
    rows, across, channels = own.shape
    step, middle = 2 * across, across // 2
    wait = copy_weights(flags, mine, theirs, weights, None, sems, None)
    for row in range(rows):
        lines = outside[row], inside[row]
        for part, line in enumerate((jnp.where(odd, lines[1], lines[0]), own[row], jnp.where(odd, lines[0], lines[1]))):
            at = (part * rows + row) * across
            upstream[at : at + across] = line
    added[...] = jnp.zeros(added.shape, F32)
    for load in loads:
        load.wait()
    contract = (((1,), (1,)), ((), ()))

    def tap_weight(layer, tap, column):
        at = (tap * 3 + column) * channels
        return weights[layer, at : at + channels, :]

    for layer in reversed(range(DEPTH)):

        def deltas(first, count, slope_ref, slope_base, layer=layer):
            @pl.loop(0, count)
            def _(index):
                base = pl.multiple_of((first + index) * across, across)
                delta = upstream[pl.ds(base, across)].astype(F32) * slope_ref[slope_base + index].astype(F32)
                spread_columns(wide, base, delta.astype(BF16).astype(F32), -1, across, channels)

        if layer == 3:
            deltas(0, rows, far_above, 0)
            deltas(rows, rows, slopes, SLOPE_BASE[3])
            deltas(2 * rows, rows, far_below, 0)
        elif layer == 2:
            deltas(1, 2, far_above, rows)
            deltas(rows - 1, rows + 2, slopes, SLOPE_BASE[2])
            deltas(2 * rows + 1, 2, far_below, rows)
        else:
            deltas(rows - 1 - layer, rows + 2 + 2 * layer, slopes, SLOPE_BASE[layer] + (2 if layer == 0 else 0))
        top, bottom = rows * across, (2 * rows - 1) * across
        wait(layer)

        def edge_terms(base, tap, layer=layer):
            for piece in range(2):
                start = base + (1 - piece) * middle
                total = None
                for column in range(3):
                    term = lax.dot_general(
                        wide[start : start + middle, column * channels : (column + 1) * channels],
                        tap_weight(layer, tap, column), contract, preferred_element_type=F32,
                    )
                    total = term if total is None else total + term
                added[base + piece * middle : base + (piece + 1) * middle, :] = total

        @pl.when(flags[0] == 1)
        def _():
            wide[top - across : top, :] = jnp.zeros((across, 3 * channels), BF16)
            edge_terms(top, 0)

        @pl.when(flags[1] == 1)
        def _():
            wide[bottom + across : bottom + 2 * across, :] = jnp.zeros((across, 3 * channels), BF16)
            edge_terms(bottom, 2)

        @pl.loop(0, rows // 2 + layer, unroll=UNROLL)
        def _(pair, layer=layer):
            row = rows - layer + 2 * pair
            base = pl.multiple_of(row * across, across)
            total = upstream[pl.ds(base, step)].astype(F32) + added[pl.ds(base, step)]
            for tap in range(3):
                for column in range(3):
                    total = total + lax.dot_general(
                        wide[pl.ds(base + (1 - tap) * across, step), column * channels : (column + 1) * channels],
                        tap_weight(layer, tap, column), contract, preferred_element_type=F32,
                    )
            upstream[pl.ds(base, step)] = total.astype(BF16)

        grads[layer] = upstream[rows * across : 2 * rows * across].reshape(rows, across, channels)
    current[...] = grads[0]

    @pl.when(block == group)
    def _():
        keep.start()
        keep.wait()


def shift(block, axis, pairs):
    return lax.ppermute(block, axis, pairs)


def on_device(fields, cotangent, kernels, biases):
    band_count = lax.axis_size("band")
    section_count = lax.axis_size("section")
    micro_count, rows, across, channels = fields.shape
    groups = section_count // DEPTH
    band = lax.axis_index("band")
    section = lax.axis_index("section")
    group = section // DEPTH
    place = section % DEPTH
    parity = band % 2
    turn = band // 2 % DEPTH
    bias = biases[0]
    high = lax.reduce_precision(bias, 8, 7)
    middle = lax.reduce_precision(bias - high, 8, 7)
    low = bias - high - middle
    extra = jnp.stack([high, middle, low] + [jnp.zeros_like(bias)] * (EXTRA - 3)).astype(BF16)

    def route(move):
        pairs = []
        for b in range(band_count):
            for s in range(section_count):
                low, y, core, z, x = b // (2 * DEPTH), b // 2 % DEPTH, b % 2, s // DEPTH, s % DEPTH
                y, core, z, x = move(y, core, z, x)
                to = (low * 2 * DEPTH + y % DEPTH * 2 + core) * section_count + z % DEPTH * DEPTH + x % DEPTH
                pairs.append((b * section_count + s, to))
        return pairs

    def carry(block, pairs):
        return lax.ppermute(block, ("band", "section"), pairs)

    def around(block, forth, back):
        middle = block.shape[0] // 2
        behind, ahead = carry(block, route(forth)), carry(block, route(back))
        return behind, ahead, carry(behind[:middle], route(forth)), carry(ahead[middle:], route(back))

    def joined(block, forth, back):
        behind, ahead, low, high = around(block, forth, back)
        return jnp.stack([block, behind, ahead, jnp.concatenate([low, high])])

    outside = [pair for i in range(1, band_count - 1, 2) for pair in ((i, i + 1), (i + 1, i))]

    partner = [(i, i ^ 1) for i in range(band_count)]

    def edges(block):
        return shift(block, "band", outside), shift(block, "band", partner)

    current, upstream = (lax.dynamic_index_in_dim(block, place, 0, keepdims=False) for block in (fields, cotangent))
    edge = jnp.concatenate([current, upstream, upstream[:2]])
    edge_outside, edge_inside = edges(edge)

    quarter = 9 * channels // 2 // DEPTH
    start = (parity * DEPTH + turn) * quarter
    piece = lax.dynamic_slice_in_dim(kernels.reshape(9 * channels, channels), start, quarter, 0)
    piece = jnp.concatenate([piece, extra])
    piece = joined(piece, lambda y, c, z, x: (y, c, z + 1, x), lambda y, c, z, x: (y, c, z - 1, x))
    piece = pl.pallas_call(
        lambda *refs: None,
        out_shape=jax.ShapeDtypeStruct(piece.shape, BF16),
        in_specs=[pl.BlockSpec(memory_space=pl.ANY)] * 3,
        out_specs=pl.BlockSpec(memory_space=pl.ANY),
        input_output_aliases={0: 0},
        name="after",
    )(piece, edge_outside, edge_inside)
    piece = joined(
        piece,
        lambda y, c, z, x: (y + c, c, z, x + 1 - c),
        lambda y, c, z, x: (y - c, c, z, x - 1 + c),
    )
    ring = around(
        piece,
        lambda y, c, z, x: (y + 1 - c, c, z, x + c),
        lambda y, c, z, x: (y - 1 + c, c, z, x - c),
    )
    mine = (piece,) + ring
    theirs = tuple(carry(block, route(lambda y, c, z, x: (y, 1 - c, z, x))) for block in mine)

    row_shape = (rows, across, channels)
    smem = pl.BlockSpec(memory_space=pltpu.SMEM)
    vmem = pl.BlockSpec(memory_space=pltpu.VMEM)
    hbm = pl.BlockSpec(memory_space=pl.ANY)
    wide = pltpu.VMEM((3 * rows * across, 3 * channels), BF16)
    weight_room = pltpu.VMEM((DEPTH, 9 * channels, channels), BF16)
    bias_room = pltpu.VMEM((DEPTH, DEPTH, EXTRA, channels), BF16)
    sems = pltpu.SemaphoreType.DMA((DEPTH, 2 * DEPTH))
    bias_sems = pltpu.SemaphoreType.DMA((DEPTH, DEPTH))
    params = pltpu.CompilerParams(vmem_limit_bytes=VMEM_LIMIT)

    def shaped(*shape):
        return jax.ShapeDtypeStruct(shape, BF16)

    cells = (across, channels)

    def flags_of(block):
        slot = (group - block) % groups
        slot = jnp.where(slot == 2, 3, jnp.where(slot == 3, 2, slot))
        return jnp.stack(
            [band == 0, band == band_count - 1, parity, turn, place, slot, block, group]
        ).astype(jnp.int32)

    forward = pl.pallas_call(
        forward_kernel,
        out_shape=(
            shaped(2 * rows + 2, *cells),
            shaped(groups, SLOPE_ROWS, *cells),
            shaped(DEPTH, *row_shape),
            shaped(groups, rows + 2, *cells),
            shaped(groups, rows + 2, *cells),
        ),
        in_specs=[smem, vmem, vmem, vmem] + [hbm] * 14,
        out_specs=(vmem,) + (hbm,) * 4,
        input_output_aliases={14: 1, 15: 2, 16: 3, 17: 4},
        scratch_shapes=[
            pltpu.VMEM((SLOPE_ROWS, *cells), BF16),
            pltpu.VMEM((DEPTH, *row_shape), BF16),
            wide,
            wide,
            weight_room,
            bias_room,
            sems,
            bias_sems,
            pltpu.SemaphoreType.DMA((4,)),
        ],
        compiler_params=params,
        name="forward",
    )
    backward = pl.pallas_call(
        backward_kernel,
        out_shape=(shaped(*row_shape), shaped(DEPTH, *row_shape)),
        in_specs=[smem] + [vmem] * 3 + [hbm] * 14,
        out_specs=(vmem, hbm),
        input_output_aliases={17: 1},
        scratch_shapes=[
            pltpu.VMEM((DEPTH, *row_shape), BF16),
            pltpu.VMEM((SLOPE_ROWS, *cells), BF16),
            pltpu.VMEM((rows + 2, *cells), BF16),
            pltpu.VMEM((rows + 2, *cells), BF16),
            pltpu.VMEM((3 * rows * across, channels), BF16),
            wide,
            pltpu.VMEM((3 * rows * across, channels), F32),
            weight_room,
            sems,
            pltpu.SemaphoreType.DMA((4,)),
        ],
        compiler_params=params,
        name="backward",
    )

    def forward_step(block, state):
        edge, outside, inside, *kept = state
        edge, *kept = forward(flags_of(block), edge, outside, inside, *mine, *theirs, *kept)
        return edge, *edges(edge), *kept

    room = pl.pallas_call(
        lambda *refs: None,
        out_shape=(
            shaped(groups, SLOPE_ROWS, *cells),
            shaped(DEPTH, *row_shape),
            shaped(groups, rows + 2, *cells),
            shaped(groups, rows + 2, *cells),
            shaped(DEPTH, *row_shape),
        ),
        out_specs=(hbm,) * 5,
        name="room",
    )()
    state = (edge, edge_outside, edge_inside, *room[:4])
    edge, above, below, slopes, states, far_above, far_below = lax.fori_loop(0, groups, forward_step, state)
    far_above = lax.dynamic_update_index_in_dim(far_above, above[rows:], groups - 1, 0)
    far_below = lax.dynamic_update_index_in_dim(far_below, below[rows:], groups - 1, 0)

    def backward_step(step, state):
        upstream, above, below, grads = state
        block = groups - 1 - step
        upstream, grads = backward(
            flags_of(block), upstream, above, below, slopes, far_above, far_below, *mine, *theirs, grads
        )
        above, below = lax.cond(block > 0, edges, lambda _: (above, below), upstream)
        return upstream, above, below, grads

    state = (upstream, edge_outside[rows : 2 * rows], edge_inside[rows : 2 * rows], room[4])
    grads = lax.fori_loop(0, groups, backward_step, state)[3]

    def deliver(kept):
        out = jnp.zeros((micro_count,) + row_shape, BF16)
        out = lax.dynamic_update_index_in_dim(out, lax.dynamic_index_in_dim(kept, place, 0, keepdims=False), place, 0)
        for step in range(1, DEPTH):
            send = lax.dynamic_index_in_dim(kept, (place + step) % DEPTH, 0, keepdims=False)
            pairs = [(g * DEPTH + p, g * DEPTH + (p + step) % DEPTH) for g in range(groups) for p in range(DEPTH)]
            received = shift(send, "section", pairs)
            out = lax.dynamic_update_index_in_dim(out, received, (place - step) % DEPTH, 0)
        return out[None]

    return deliver(states), deliver(grads)


def solution(mesh):
    placed = (
        P(None, "band", None, None),
        P(None, "band", None, None),
        P("section", None, None, None, None),
        P("section", None),
    )
    return jax.shard_map(
        on_device,
        mesh=mesh,
        in_specs=placed,
        out_specs=(P("section", None, "band", None, None), P("section", None, "band", None, None)),
        check_vma=False,
    )
```

```python
import jax
import jax.numpy as jnp
from jax import lax
from jax.experimental import pallas as pl
from jax.experimental.pallas import tpu as pltpu
from jax.sharding import PartitionSpec as P


DEPTH = 4
CHUNKS = (1, 2)
EXTRA = 16
SLOPE_BASE = (0, 10, 18, 24)
SLOPE_ROWS = 28
VMEM_LIMIT = 52 * 1024 * 1024
BF16 = jnp.bfloat16
F32 = jnp.float32


def spread_columns(ref, base, value, shift, across, channels):
    count = value.shape[0]
    cells = value.reshape(count // across, across, channels)
    before = pltpu.roll(cells, shift % across, 1).reshape(count, channels)
    after = pltpu.roll(cells, -shift % across, 1).reshape(count, channels)
    ref[pl.ds(base, count), 0:channels] = before.astype(BF16)
    ref[pl.ds(base, count), channels : 2 * channels] = value.astype(BF16)
    ref[pl.ds(base, count), 2 * channels : 3 * channels] = after.astype(BF16)


def copy_weights(flags, mine, theirs, weights, bias, sems, bias_sems):
    parity, turn, place = flags[2], flags[3], flags[4]
    rows = weights.shape[1] // (2 * DEPTH)
    slot = flags[5]
    behind = (0, 1, 3, 2)
    for side, pieces in enumerate((mine, theirs)):
        core = parity if side == 0 else 1 - parity
        for outer in range(DEPTH):
            for inner in range(DEPTH):
                source = pieces[outer] if outer < 3 else pieces[3 + inner // 2]
                index = inner if outer < 3 else inner % 2
                first, second = behind[inner], behind[outer]
                layer = (place - jnp.where(core == 0, first, second) + DEPTH) % DEPTH
                part = (turn - jnp.where(core == 0, second, first) + DEPTH) % DEPTH
                at = core * DEPTH + part
                pltpu.make_async_copy(
                    source.at[index, slot, pl.ds(0, rows)],
                    weights.at[layer, pl.ds(pl.multiple_of(at * rows, 32), rows)],
                    sems.at[layer, at],
                ).start()
                if side == 0 and bias is not None:
                    pltpu.make_async_copy(
                        source.at[index, slot, pl.ds(rows, EXTRA)], bias.at[layer, part], bias_sems.at[layer, part]
                    ).start()

    def wait(layer):
        for at in range(2 * DEPTH):
            pltpu.make_async_copy(
                mine[0].at[0, 0, pl.ds(0, rows)], weights.at[layer, pl.ds(at * rows, rows)], sems.at[layer, at]
            ).wait()
        if bias is not None:
            for part in range(DEPTH):
                pltpu.make_async_copy(
                    mine[0].at[0, 0, pl.ds(rows, EXTRA)], bias.at[layer, part], bias_sems.at[layer, part]
                ).wait()

    return wait


def forward_kernel(flags, own, outside, inside, *refs):
    mine, theirs = refs[:5], refs[5:10]
    edge, all_slopes, kept_states, all_outside, all_inside = refs[14:19]
    slopes, states, wide, other, weights, bias, sems, bias_sems, out_sems = refs[19:]
    block, group = flags[6], flags[7]
    save = pltpu.make_async_copy(slopes, all_slopes.at[block], out_sems.at[0])
    keep = pltpu.make_async_copy(states, kept_states, out_sems.at[1])
    rows, across, channels = states.shape[1:]
    wait = copy_weights(flags, mine, theirs, weights, bias, sems, bias_sems)
    last_block = (block + DEPTH - 1) % DEPTH
    pass_on = [
        pltpu.make_async_copy(piece.at[pl.ds(rows, rows + 2)], kept.at[last_block], out_sems.at[2 + index])
        for index, (piece, kept) in enumerate(((outside, all_outside), (inside, all_inside)))
    ]
    for copy in pass_on:
        copy.start()
    odd = flags[2] == 1
    for part in range(3):

        @pl.loop(0, rows)
        def _(row, part=part):
            base = pl.multiple_of((part * rows + row) * across, across)
            if part == 1:
                line = own[row].astype(F32)
            else:
                pair = (inside, outside) if part == 0 else (outside, inside)
                line = jnp.where(odd, pair[0][row].astype(F32), pair[1][row].astype(F32))
            spread_columns(wide, base, line, 1, across, channels)

    def poles(ref):
        middle = across // 2
        top, bottom = rows * across, (2 * rows - 1) * across

        @pl.when(flags[0] == 1)
        def _():
            ref[top - across : top - middle, :] = ref[top + middle : top + across, :]
            ref[top - middle : top, :] = ref[top : top + middle, :]

        @pl.when(flags[1] == 1)
        def _():
            ref[bottom + across : bottom + across + middle, :] = ref[bottom + middle : bottom + across, :]
            ref[bottom + across + middle : bottom + 2 * across, :] = ref[bottom : bottom + middle, :]

    for layer in range(DEPTH):
        source, target = (wide, other) if layer % 2 == 0 else (other, wide)
        poles(source)
        wait(layer)
        reach = DEPTH - 1 - layer
        parts = bias[layer, 0].astype(F32)
        offset = (parts[0:1] + parts[1:2]) + parts[2:3]

        height = rows + 2 * reach
        for index in range(0, height, CHUNKS[0]):
            count = min(CHUNKS[0], height - index)
            step = count * across
            base = (rows - reach + index) * across
            preact = None
            for tap in range(3):
                term = jnp.dot(
                    source[pl.ds(base + (tap - 1) * across, step), :],
                    weights[layer, tap * 3 * channels : (tap + 1) * 3 * channels, :],
                    preferred_element_type=F32,
                )
                preact = term if preact is None else preact + term
            preact = preact + offset
            sigmoid = 0.5 * jnp.tanh(0.5 * preact) + 0.5
            silu = preact * sigmoid
            slope = (sigmoid + silu * (1.0 - sigmoid)).astype(BF16).reshape(count, across, channels)
            before = source[pl.ds(base, step), channels : 2 * channels].astype(F32)
            result = (before + silu).astype(BF16)
            if layer < DEPTH - 1:
                spread_columns(target, base, result.astype(F32), 1, across, channels)
            slopes[pl.ds(SLOPE_BASE[layer] + index, count)] = slope
            if layer == DEPTH - 1:
                edge[pl.ds(index, count)] = result.reshape(count, across, channels)

        if layer < DEPTH - 1:
            own_cells = target[rows * across : 2 * rows * across, channels : 2 * channels]
            states[layer] = own_cells.reshape(rows, across, channels)
    states[DEPTH - 1] = edge[0:rows]
    edge[rows : 2 * rows] = slopes[SLOPE_BASE[3] : SLOPE_BASE[3] + rows]
    edge[2 * rows :] = slopes[SLOPE_BASE[2] + 2 : SLOPE_BASE[2] + 4]
    save.start()

    @pl.when(block == group)
    def _():
        keep.start()
        keep.wait()

    for copy in [save] + pass_on:
        copy.wait()


def backward_kernel(flags, own, outside, inside, all_slopes, all_outside, all_inside, last_outside, last_inside, *refs):
    mine, theirs = refs[:5], refs[5:10]
    rows = own.shape[0]
    current, kept_grads = refs[11:13]
    grads, slopes, far_above, far_below, upstream, wide, added, weights, sems, out_sems = refs[13:]
    block, group = flags[6], flags[7]
    odd = flags[2] == 1
    for swapped in range(2):

        @pl.when((flags[2] == swapped) & (block < DEPTH - 1))
        def _(swapped=swapped):
            ends = (all_inside, all_outside) if swapped else (all_outside, all_inside)
            for index, (source, target) in enumerate(zip(ends, (far_above, far_below))):
                pltpu.make_async_copy(source.at[block], target, out_sems.at[index]).start()

        @pl.when((flags[2] == swapped) & (block == DEPTH - 1))
        def _(swapped=swapped):
            ends = (last_inside, last_outside) if swapped else (last_outside, last_inside)
            for index, (source, target) in enumerate(zip(ends, (far_above, far_below))):
                pltpu.make_async_copy(source.at[pl.ds(rows, rows + 2)], target, out_sems.at[index]).start()

    pltpu.make_async_copy(all_slopes.at[block], slopes, out_sems.at[2]).start()
    loads = [
        pltpu.make_async_copy(source.at[block], target, out_sems.at[index])
        for index, (source, target) in enumerate(
            ((all_outside, far_above), (all_inside, far_below), (all_slopes, slopes))
        )
    ]
    keep = pltpu.make_async_copy(grads, kept_grads, out_sems.at[3])
    rows, across, channels = own.shape
    middle = across // 2
    wait = copy_weights(flags, mine, theirs, weights, None, sems, None)
    for row in range(rows):
        lines = outside[row], inside[row]
        for part, line in enumerate((jnp.where(odd, lines[1], lines[0]), own[row], jnp.where(odd, lines[0], lines[1]))):
            at = (part * rows + row) * across
            upstream[at : at + across] = line
    added[...] = jnp.zeros(added.shape, F32)
    for load in loads:
        load.wait()
    contract = (((1,), (1,)), ((), ()))

    def tap_weight(layer, tap, column):
        at = (tap * 3 + column) * channels
        return weights[layer, at : at + channels, :]

    for layer in reversed(range(DEPTH)):

        def deltas(first, count, slope_ref, slope_base):
            @pl.loop(0, count)
            def _(index):
                base = pl.multiple_of((first + index) * across, across)
                delta = upstream[pl.ds(base, across)].astype(F32) * slope_ref[slope_base + index].astype(F32)
                spread_columns(wide, base, delta.astype(BF16).astype(F32), -1, across, channels)

        if layer == 3:
            deltas(0, rows, far_above, 0)
            deltas(rows, rows, slopes, SLOPE_BASE[3])
            deltas(2 * rows, rows, far_below, 0)
        elif layer == 2:
            deltas(1, 2, far_above, rows)
            deltas(rows - 1, rows + 2, slopes, SLOPE_BASE[2])
            deltas(2 * rows + 1, 2, far_below, rows)
        else:
            deltas(rows - 1 - layer, rows + 2 + 2 * layer, slopes, SLOPE_BASE[layer] + (2 if layer == 0 else 0))
        top, bottom = rows * across, (2 * rows - 1) * across
        wait(layer)

        def edge_terms(base, tap, layer=layer):
            for piece in range(2):
                start = base + (1 - piece) * middle
                total = None
                for column in range(3):
                    term = lax.dot_general(
                        wide[start : start + middle, column * channels : (column + 1) * channels],
                        tap_weight(layer, tap, column), contract, preferred_element_type=F32,
                    )
                    total = term if total is None else total + term
                added[base + piece * middle : base + (piece + 1) * middle, :] = total

        @pl.when(flags[0] == 1)
        def _():
            wide[top - across : top, :] = jnp.zeros((across, 3 * channels), BF16)
            edge_terms(top, 0)

        @pl.when(flags[1] == 1)
        def _():
            wide[bottom + across : bottom + 2 * across, :] = jnp.zeros((across, 3 * channels), BF16)
            edge_terms(bottom, 2)

        height = rows + 2 * layer
        for index in range(0, height, CHUNKS[1]):
            count = min(CHUNKS[1], height - index)
            step = count * across
            base = (rows - layer + index) * across
            total = upstream[pl.ds(base, step)].astype(F32) + added[pl.ds(base, step)]
            for tap in range(3):
                for column in range(3):
                    total = total + lax.dot_general(
                        wide[pl.ds(base + (1 - tap) * across, step), column * channels : (column + 1) * channels],
                        tap_weight(layer, tap, column), contract, preferred_element_type=F32,
                    )
            upstream[pl.ds(base, step)] = total.astype(BF16)

        grads[layer] = upstream[rows * across : 2 * rows * across].reshape(rows, across, channels)
    current[...] = grads[0]

    @pl.when(block == group)
    def _():
        keep.start()
        keep.wait()


def shift(block, axis, pairs):
    return lax.ppermute(block, axis, pairs)


def on_device(fields, cotangent, kernels, biases):
    band_count = lax.axis_size("band")
    section_count = lax.axis_size("section")
    micro_count, rows, across, channels = fields.shape
    groups = section_count // DEPTH
    band = lax.axis_index("band")
    section = lax.axis_index("section")
    group = section // DEPTH
    place = section % DEPTH
    parity = band % 2
    turn = band // 2 % DEPTH
    bias = biases[0]
    high = lax.reduce_precision(bias, 8, 7)
    middle = lax.reduce_precision(bias - high, 8, 7)
    low = bias - high - middle
    extra = jnp.stack([high, middle, low] + [jnp.zeros_like(bias)] * (EXTRA - 3)).astype(BF16)

    def route(move):
        pairs = []
        for b in range(band_count):
            for s in range(section_count):
                low, y, core, z, x = b // (2 * DEPTH), b // 2 % DEPTH, b % 2, s // DEPTH, s % DEPTH
                y, core, z, x = move(y, core, z, x)
                to = (low * 2 * DEPTH + y % DEPTH * 2 + core) * section_count + z % DEPTH * DEPTH + x % DEPTH
                pairs.append((b * section_count + s, to))
        return pairs

    def carry(block, pairs):
        return lax.ppermute(block, ("band", "section"), pairs)

    def around(block, forth, back):
        middle = block.shape[0] // 2
        behind, ahead = carry(block, route(forth)), carry(block, route(back))
        return behind, ahead, carry(behind[:middle], route(forth)), carry(ahead[middle:], route(back))

    def joined(block, forth, back):
        behind, ahead, low, high = around(block, forth, back)
        return jnp.stack([block, behind, ahead, jnp.concatenate([low, high])])

    outside = [pair for i in range(1, band_count - 1, 2) for pair in ((i, i + 1), (i + 1, i))]

    partner = [(i, i ^ 1) for i in range(band_count)]

    def edges(block):
        return shift(block, "band", outside), shift(block, "band", partner)

    current, upstream = (lax.dynamic_index_in_dim(block, place, 0, keepdims=False) for block in (fields, cotangent))
    edge = jnp.concatenate([current, upstream, upstream[:2]])

    quarter = 9 * channels // 2 // DEPTH
    start = (parity * DEPTH + turn) * quarter
    piece = lax.dynamic_slice_in_dim(kernels.reshape(9 * channels, channels), start, quarter, 0)
    piece = jnp.concatenate([piece, extra])
    hbm = pl.BlockSpec(memory_space=pl.ANY)

    def after(block, *others):
        return pl.pallas_call(
            lambda *refs: None,
            out_shape=jax.ShapeDtypeStruct(block.shape, BF16),
            in_specs=[hbm] * (1 + len(others)),
            out_specs=hbm,
            input_output_aliases={0: 0},
            name="after",
        )(block, *others)

    forth, back = route(lambda y, c, z, x: (y, c, z + 1, x)), route(lambda y, c, z, x: (y, c, z - 1, x))
    behind, ahead = carry(piece, forth), carry(piece, back)
    low, high = carry(behind[: (quarter + EXTRA) // 2], forth), carry(ahead[(quarter + EXTRA) // 2 :], back)
    edge = after(edge, behind)
    edge_outside, edge_inside = edges(edge)

    def take_edges(piece, outside, inside, out, first, second, sems):
        copies = [
            pltpu.make_async_copy(source.at[pl.ds(rows, rows)], target, sems.at[index])
            for index, (source, target) in enumerate(((outside, first), (inside, second)))
        ]
        for copy in copies:
            copy.start()
        for copy in copies:
            copy.wait()

    piece = jnp.stack([piece, behind, ahead, jnp.concatenate([low, high])])
    part_shape = jax.ShapeDtypeStruct((rows, across, channels), BF16)
    piece, start_outside, start_inside = pl.pallas_call(
        take_edges,
        out_shape=(jax.ShapeDtypeStruct(piece.shape, BF16), part_shape, part_shape),
        in_specs=[hbm] * 3,
        out_specs=(hbm,) * 3,
        input_output_aliases={0: 0},
        scratch_shapes=[pltpu.SemaphoreType.DMA((2,))],
        name="take_edges",
    )(piece, edge_outside, edge_inside)
    piece = joined(
        piece,
        lambda y, c, z, x: (y + c, c, z, x + 1 - c),
        lambda y, c, z, x: (y - c, c, z, x - 1 + c),
    )
    ring = around(
        piece,
        lambda y, c, z, x: (y + 1 - c, c, z, x + c),
        lambda y, c, z, x: (y - 1 + c, c, z, x - c),
    )
    mine = (piece,) + ring
    theirs = tuple(carry(block, route(lambda y, c, z, x: (y, 1 - c, z, x))) for block in mine)

    row_shape = (rows, across, channels)
    smem = pl.BlockSpec(memory_space=pltpu.SMEM)
    vmem = pl.BlockSpec(memory_space=pltpu.VMEM)
    hbm = pl.BlockSpec(memory_space=pl.ANY)
    wide = pltpu.VMEM((3 * rows * across, 3 * channels), BF16)
    weight_room = pltpu.VMEM((DEPTH, 9 * channels, channels), BF16)
    bias_room = pltpu.VMEM((DEPTH, DEPTH, EXTRA, channels), BF16)
    sems = pltpu.SemaphoreType.DMA((DEPTH, 2 * DEPTH))
    bias_sems = pltpu.SemaphoreType.DMA((DEPTH, DEPTH))
    params = pltpu.CompilerParams(vmem_limit_bytes=VMEM_LIMIT)

    def shaped(*shape):
        return jax.ShapeDtypeStruct(shape, BF16)

    cells = (across, channels)

    def flags_of(block):
        slot = (group - block) % groups
        slot = jnp.where(slot == 2, 3, jnp.where(slot == 3, 2, slot))
        return jnp.stack(
            [band == 0, band == band_count - 1, parity, turn, place, slot, block, group]
        ).astype(jnp.int32)

    forward = pl.pallas_call(
        forward_kernel,
        out_shape=(
            shaped(2 * rows + 2, *cells),
            shaped(groups, SLOPE_ROWS, *cells),
            shaped(DEPTH, *row_shape),
            shaped(groups, rows + 2, *cells),
            shaped(groups, rows + 2, *cells),
        ),
        in_specs=[smem, vmem, vmem, vmem] + [hbm] * 14,
        out_specs=(vmem,) + (hbm,) * 4,
        input_output_aliases={14: 1, 15: 2, 16: 3, 17: 4},
        scratch_shapes=[
            pltpu.VMEM((SLOPE_ROWS, *cells), BF16),
            pltpu.VMEM((DEPTH, *row_shape), BF16),
            wide,
            wide,
            weight_room,
            bias_room,
            sems,
            bias_sems,
            pltpu.SemaphoreType.DMA((4,)),
        ],
        compiler_params=params,
        name="forward",
    )
    backward = pl.pallas_call(
        backward_kernel,
        out_shape=(shaped(*row_shape), shaped(DEPTH, *row_shape)),
        in_specs=[smem] + [vmem] * 3 + [hbm] * 16,
        out_specs=(vmem, hbm),
        input_output_aliases={19: 1},
        scratch_shapes=[
            pltpu.VMEM((DEPTH, *row_shape), BF16),
            pltpu.VMEM((SLOPE_ROWS, *cells), BF16),
            pltpu.VMEM((rows + 2, *cells), BF16),
            pltpu.VMEM((rows + 2, *cells), BF16),
            pltpu.VMEM((3 * rows * across, channels), BF16),
            wide,
            pltpu.VMEM((3 * rows * across, channels), F32),
            weight_room,
            sems,
            pltpu.SemaphoreType.DMA((4,)),
        ],
        compiler_params=params,
        name="backward",
    )

    def forward_step(block, state):
        edge, outside, inside, *kept = state
        edge, *kept = forward(flags_of(block), edge, outside, inside, *mine, *theirs, *kept)
        return edge, *edges(edge), *kept

    room = pl.pallas_call(
        lambda *refs: None,
        out_shape=(
            shaped(groups, SLOPE_ROWS, *cells),
            shaped(DEPTH, *row_shape),
            shaped(groups, rows + 2, *cells),
            shaped(groups, rows + 2, *cells),
            shaped(DEPTH, *row_shape),
        ),
        out_specs=(hbm,) * 5,
        name="room",
    )()
    state = (edge, edge_outside, edge_inside, *room[:4])
    edge, last_outside, last_inside, slopes, states, far_outside, far_inside = lax.fori_loop(
        0, groups, forward_step, state
    )

    def deliver(kept):
        out = jnp.zeros((micro_count,) + row_shape, BF16)
        out = lax.dynamic_update_index_in_dim(out, lax.dynamic_index_in_dim(kept, place, 0, keepdims=False), place, 0)
        for step in range(1, DEPTH):
            send = lax.dynamic_index_in_dim(kept, (place + step) % DEPTH, 0, keepdims=False)
            pairs = [(g * DEPTH + p, g * DEPTH + (p + step) % DEPTH) for g in range(groups) for p in range(DEPTH)]
            received = shift(send, "section", pairs)
            out = lax.dynamic_update_index_in_dim(out, received, (place - step) % DEPTH, 0)
        return out[None]

    delivered = deliver(states)

    def backward_step(step, state):
        upstream, above, below, grads = state
        block = groups - 1 - step
        upstream, grads = backward(
            flags_of(block), upstream, above, below, slopes, far_outside, far_inside, last_outside, last_inside,
            *mine, *theirs, grads,
        )
        above, below = lax.cond(block > 0, edges, lambda _: (above, below), upstream)
        return upstream, above, below, grads

    state = (upstream, start_outside, start_inside, room[4])
    grads = lax.fori_loop(0, groups, backward_step, state)[3]

    return delivered, deliver(grads)


def solution(mesh):
    placed = (
        P(None, "band", None, None),
        P(None, "band", None, None),
        P("section", None, None, None, None),
        P("section", None),
    )
    return jax.shard_map(
        on_device,
        mesh=mesh,
        in_specs=placed,
        out_specs=(P("section", None, "band", None, None), P("section", None, "band", None, None)),
        check_vma=False,
    )
```

```python
import jax
import jax.numpy as jnp
from jax import lax
from jax.experimental import pallas as pl
from jax.experimental.pallas import tpu as pltpu
from jax.sharding import PartitionSpec as P


DEPTH = 4
CHUNKS = (1, 2)
EXTRA = 16
SLOPE_BASE = (0, 10, 18, 24)
SLOPE_ROWS = 28
VMEM_LIMIT = 52 * 1024 * 1024
BF16 = jnp.bfloat16
F32 = jnp.float32


def spread_columns(ref, base, value, shift, across, channels):
    count = value.shape[0]
    cells = value.reshape(count // across, across, channels)
    before = pltpu.roll(cells, shift % across, 1).reshape(count, channels)
    after = pltpu.roll(cells, -shift % across, 1).reshape(count, channels)
    ref[pl.ds(base, count), 0:channels] = before.astype(BF16)
    ref[pl.ds(base, count), channels : 2 * channels] = value.astype(BF16)
    ref[pl.ds(base, count), 2 * channels : 3 * channels] = after.astype(BF16)


def copy_weights(flags, mine, theirs, weights, bias, sems, bias_sems):
    parity, turn, place = flags[2], flags[3], flags[4]
    rows = weights.shape[1] // (2 * DEPTH)
    slot = flags[5]
    behind = (0, 1, 3, 2)
    for side, pieces in enumerate((mine, theirs)):
        core = parity if side == 0 else 1 - parity
        for outer in range(DEPTH):
            for inner in range(DEPTH):
                source = pieces[outer] if outer < 3 else pieces[3 + inner // 2]
                index = inner if outer < 3 else inner % 2
                first, second = behind[inner], behind[outer]
                layer = (place - jnp.where(core == 0, first, second) + DEPTH) % DEPTH
                part = (turn - jnp.where(core == 0, second, first) + DEPTH) % DEPTH
                at = core * DEPTH + part
                pltpu.make_async_copy(
                    source.at[index, slot, pl.ds(0, rows)],
                    weights.at[layer, pl.ds(pl.multiple_of(at * rows, 32), rows)],
                    sems.at[layer, at],
                ).start()
                if side == 0 and bias is not None:
                    pltpu.make_async_copy(
                        source.at[index, slot, pl.ds(rows, EXTRA)], bias.at[layer, part], bias_sems.at[layer, part]
                    ).start()

    def wait(layer):
        for at in range(2 * DEPTH):
            pltpu.make_async_copy(
                mine[0].at[0, 0, pl.ds(0, rows)], weights.at[layer, pl.ds(at * rows, rows)], sems.at[layer, at]
            ).wait()
        if bias is not None:
            for part in range(DEPTH):
                pltpu.make_async_copy(
                    mine[0].at[0, 0, pl.ds(rows, EXTRA)], bias.at[layer, part], bias_sems.at[layer, part]
                ).wait()

    return wait


def forward_kernel(flags, own, outside, inside, *refs):
    mine, theirs = refs[:5], refs[5:10]
    edge, all_slopes, kept_states, all_outside, all_inside = refs[14:19]
    slopes, states, wide, other, weights, bias, sems, bias_sems, out_sems = refs[19:]
    block, group = flags[6], flags[7]
    save = pltpu.make_async_copy(slopes, all_slopes.at[block], out_sems.at[0])
    keep = pltpu.make_async_copy(states, kept_states, out_sems.at[1])
    rows, across, channels = states.shape[1:]
    wait = copy_weights(flags, mine, theirs, weights, bias, sems, bias_sems)
    last_block = (block + DEPTH - 1) % DEPTH
    pass_on = [
        pltpu.make_async_copy(piece.at[pl.ds(rows, rows + 2)], kept.at[last_block], out_sems.at[2 + index])
        for index, (piece, kept) in enumerate(((outside, all_outside), (inside, all_inside)))
    ]
    for copy in pass_on:
        copy.start()
    odd = flags[2] == 1
    for part in range(3):

        @pl.loop(0, rows)
        def _(row, part=part):
            base = pl.multiple_of((part * rows + row) * across, across)
            if part == 1:
                line = own[row].astype(F32)
            else:
                pair = (inside, outside) if part == 0 else (outside, inside)
                line = jnp.where(odd, pair[0][row].astype(F32), pair[1][row].astype(F32))
            spread_columns(wide, base, line, 1, across, channels)

    def poles(ref):
        middle = across // 2
        top, bottom = rows * across, (2 * rows - 1) * across

        @pl.when(flags[0] == 1)
        def _():
            ref[top - across : top - middle, :] = ref[top + middle : top + across, :]
            ref[top - middle : top, :] = ref[top : top + middle, :]

        @pl.when(flags[1] == 1)
        def _():
            ref[bottom + across : bottom + across + middle, :] = ref[bottom + middle : bottom + across, :]
            ref[bottom + across + middle : bottom + 2 * across, :] = ref[bottom : bottom + middle, :]

    for layer in range(DEPTH):
        source, target = (wide, other) if layer % 2 == 0 else (other, wide)
        poles(source)
        wait(layer)
        reach = DEPTH - 1 - layer
        parts = bias[layer, 0].astype(F32)
        offset = (parts[0:1] + parts[1:2]) + parts[2:3]

        height = rows + 2 * reach
        for index in range(0, height, CHUNKS[0]):
            count = min(CHUNKS[0], height - index)
            step = count * across
            base = (rows - reach + index) * across
            preact = None
            for tap in range(3):
                term = jnp.dot(
                    source[pl.ds(base + (tap - 1) * across, step), :],
                    weights[layer, tap * 3 * channels : (tap + 1) * 3 * channels, :],
                    preferred_element_type=F32,
                )
                preact = term if preact is None else preact + term
            preact = preact + offset
            sigmoid = 0.5 * jnp.tanh(0.5 * preact) + 0.5
            silu = preact * sigmoid
            slope = (sigmoid + silu * (1.0 - sigmoid)).astype(BF16).reshape(count, across, channels)
            before = source[pl.ds(base, step), channels : 2 * channels].astype(F32)
            result = (before + silu).astype(BF16)
            if layer < DEPTH - 1:
                spread_columns(target, base, result.astype(F32), 1, across, channels)
            slopes[pl.ds(SLOPE_BASE[layer] + index, count)] = slope
            if layer == DEPTH - 1:
                edge[pl.ds(index, count)] = result.reshape(count, across, channels)

        if layer < DEPTH - 1:
            own_cells = target[rows * across : 2 * rows * across, channels : 2 * channels]
            states[layer] = own_cells.reshape(rows, across, channels)
    states[DEPTH - 1] = edge[0:rows]
    edge[rows : 2 * rows] = slopes[SLOPE_BASE[3] : SLOPE_BASE[3] + rows]
    edge[2 * rows :] = slopes[SLOPE_BASE[2] + 2 : SLOPE_BASE[2] + 4]
    save.start()

    @pl.when(block == group)
    def _():
        keep.start()
        keep.wait()

    for copy in [save] + pass_on:
        copy.wait()


def backward_kernel(flags, own, outside, inside, all_slopes, all_outside, all_inside, last_outside, last_inside, *refs):
    mine, theirs = refs[:5], refs[5:10]
    rows = own.shape[0]
    current, kept_grads = refs[11:13]
    grads, slopes, far_above, far_below, upstream, wide, added, weights, sems, out_sems = refs[13:]
    block, group = flags[6], flags[7]
    odd = flags[2] == 1
    for swapped in range(2):

        @pl.when((flags[2] == swapped) & (block < DEPTH - 1))
        def _(swapped=swapped):
            ends = (all_inside, all_outside) if swapped else (all_outside, all_inside)
            for index, (source, target) in enumerate(zip(ends, (far_above, far_below))):
                pltpu.make_async_copy(source.at[block], target, out_sems.at[index]).start()

        @pl.when((flags[2] == swapped) & (block == DEPTH - 1))
        def _(swapped=swapped):
            ends = (last_inside, last_outside) if swapped else (last_outside, last_inside)
            for index, (source, target) in enumerate(zip(ends, (far_above, far_below))):
                pltpu.make_async_copy(source.at[pl.ds(rows, rows + 2)], target, out_sems.at[index]).start()

    pltpu.make_async_copy(all_slopes.at[block], slopes, out_sems.at[2]).start()
    loads = [
        pltpu.make_async_copy(source.at[block], target, out_sems.at[index])
        for index, (source, target) in enumerate(
            ((all_outside, far_above), (all_inside, far_below), (all_slopes, slopes))
        )
    ]
    keep = pltpu.make_async_copy(grads, kept_grads, out_sems.at[3])
    rows, across, channels = own.shape
    middle = across // 2
    wait = copy_weights(flags, mine, theirs, weights, None, sems, None)
    for row in range(rows):
        lines = outside[row], inside[row]
        for part, line in enumerate((jnp.where(odd, lines[1], lines[0]), own[row], jnp.where(odd, lines[0], lines[1]))):
            at = (part * rows + row) * across
            upstream[at : at + across] = line
    added[...] = jnp.zeros(added.shape, F32)
    for load in loads:
        load.wait()
    contract = (((1,), (1,)), ((), ()))

    def tap_weight(layer, tap, column):
        at = (tap * 3 + column) * channels
        return weights[layer, at : at + channels, :]

    for layer in reversed(range(DEPTH)):

        def deltas(first, count, slope_ref, slope_base):
            @pl.loop(0, count)
            def _(index):
                base = pl.multiple_of((first + index) * across, across)
                delta = upstream[pl.ds(base, across)].astype(F32) * slope_ref[slope_base + index].astype(F32)
                spread_columns(wide, base, delta.astype(BF16).astype(F32), -1, across, channels)

        if layer == 3:
            deltas(0, rows, far_above, 0)
            deltas(rows, rows, slopes, SLOPE_BASE[3])
            deltas(2 * rows, rows, far_below, 0)
        elif layer == 2:
            deltas(1, 2, far_above, rows)
            deltas(rows - 1, rows + 2, slopes, SLOPE_BASE[2])
            deltas(2 * rows + 1, 2, far_below, rows)
        else:
            deltas(rows - 1 - layer, rows + 2 + 2 * layer, slopes, SLOPE_BASE[layer] + (2 if layer == 0 else 0))
        top, bottom = rows * across, (2 * rows - 1) * across
        wait(layer)

        def edge_terms(base, tap, layer=layer):
            for piece in range(2):
                start = base + (1 - piece) * middle
                total = None
                for column in range(3):
                    term = lax.dot_general(
                        wide[start : start + middle, column * channels : (column + 1) * channels],
                        tap_weight(layer, tap, column), contract, preferred_element_type=F32,
                    )
                    total = term if total is None else total + term
                added[base + piece * middle : base + (piece + 1) * middle, :] = total

        @pl.when(flags[0] == 1)
        def _():
            wide[top - across : top, :] = jnp.zeros((across, 3 * channels), BF16)
            edge_terms(top, 0)

        @pl.when(flags[1] == 1)
        def _():
            wide[bottom + across : bottom + 2 * across, :] = jnp.zeros((across, 3 * channels), BF16)
            edge_terms(bottom, 2)

        height = rows + 2 * layer
        for index in range(0, height, CHUNKS[1]):
            count = min(CHUNKS[1], height - index)
            step = count * across
            base = (rows - layer + index) * across
            total = upstream[pl.ds(base, step)].astype(F32) + added[pl.ds(base, step)]
            for tap in range(3):
                for column in range(3):
                    total = total + lax.dot_general(
                        wide[pl.ds(base + (1 - tap) * across, step), column * channels : (column + 1) * channels],
                        tap_weight(layer, tap, column), contract, preferred_element_type=F32,
                    )
            upstream[pl.ds(base, step)] = total.astype(BF16)

        grads[layer] = upstream[rows * across : 2 * rows * across].reshape(rows, across, channels)
    current[...] = grads[0]

    @pl.when(block == group)
    def _():
        keep.start()
        keep.wait()


def shift(block, axis, pairs):
    return lax.ppermute(block, axis, pairs)


def on_device(fields, cotangent, kernels, biases):
    band_count = lax.axis_size("band")
    section_count = lax.axis_size("section")
    micro_count, rows, across, channels = fields.shape
    groups = section_count // DEPTH
    band = lax.axis_index("band")
    section = lax.axis_index("section")
    group = section // DEPTH
    place = section % DEPTH
    parity = band % 2
    turn = band // 2 % DEPTH
    bias = biases[0]
    high = lax.reduce_precision(bias, 8, 7)
    middle = lax.reduce_precision(bias - high, 8, 7)
    low = bias - high - middle
    extra = jnp.stack([high, middle, low] + [jnp.zeros_like(bias)] * (EXTRA - 3)).astype(BF16)

    def route(move):
        pairs = []
        for b in range(band_count):
            for s in range(section_count):
                low, y, core, z, x = b // (2 * DEPTH), b // 2 % DEPTH, b % 2, s // DEPTH, s % DEPTH
                y, core, z, x = move(y, core, z, x)
                to = (low * 2 * DEPTH + y % DEPTH * 2 + core) * section_count + z % DEPTH * DEPTH + x % DEPTH
                pairs.append((b * section_count + s, to))
        return pairs

    def carry(block, pairs):
        return lax.ppermute(block, ("band", "section"), pairs)

    def around(block, forth, back):
        middle = block.shape[0] // 2
        behind, ahead = carry(block, route(forth)), carry(block, route(back))
        return behind, ahead, carry(behind[:middle], route(forth)), carry(ahead[middle:], route(back))

    def joined(block, forth, back):
        behind, ahead, low, high = around(block, forth, back)
        return jnp.stack([block, behind, ahead, jnp.concatenate([low, high])])

    outside = [pair for i in range(1, band_count - 1, 2) for pair in ((i, i + 1), (i + 1, i))]

    partner = [(i, i ^ 1) for i in range(band_count)]

    def edges(block):
        return shift(block, "band", outside), shift(block, "band", partner)

    current, upstream = (lax.dynamic_index_in_dim(block, place, 0, keepdims=False) for block in (fields, cotangent))
    edge = jnp.concatenate([current, upstream, upstream[:2]])

    quarter = 9 * channels // 2 // DEPTH
    start = (parity * DEPTH + turn) * quarter
    piece = lax.dynamic_slice_in_dim(kernels.reshape(9 * channels, channels), start, quarter, 0)
    piece = jnp.concatenate([piece, extra])
    hbm = pl.BlockSpec(memory_space=pl.ANY)
    vmem = pl.BlockSpec(memory_space=pltpu.VMEM)
    edge_outside, edge_inside = edges(edge)
    piece = joined(piece, lambda y, c, z, x: (y, c, z + 1, x), lambda y, c, z, x: (y, c, z - 1, x))

    def take_edges(piece, outside, inside, out, first, second):
        first[...] = outside[rows : 2 * rows]
        second[...] = inside[rows : 2 * rows]

    part_shape = jax.ShapeDtypeStruct((rows, across, channels), BF16)
    piece, start_outside, start_inside = pl.pallas_call(
        take_edges,
        out_shape=(jax.ShapeDtypeStruct(piece.shape, BF16), part_shape, part_shape),
        in_specs=[hbm, vmem, vmem],
        out_specs=(hbm, vmem, vmem),
        input_output_aliases={0: 0},
        name="take_edges",
    )(piece, edge_outside, edge_inside)
    piece = joined(
        piece,
        lambda y, c, z, x: (y + c, c, z, x + 1 - c),
        lambda y, c, z, x: (y - c, c, z, x - 1 + c),
    )
    ring = around(
        piece,
        lambda y, c, z, x: (y + 1 - c, c, z, x + c),
        lambda y, c, z, x: (y - 1 + c, c, z, x - c),
    )
    mine = (piece,) + ring
    theirs = tuple(carry(block, route(lambda y, c, z, x: (y, 1 - c, z, x))) for block in mine)

    row_shape = (rows, across, channels)
    smem = pl.BlockSpec(memory_space=pltpu.SMEM)
    vmem = pl.BlockSpec(memory_space=pltpu.VMEM)
    hbm = pl.BlockSpec(memory_space=pl.ANY)
    wide = pltpu.VMEM((3 * rows * across, 3 * channels), BF16)
    weight_room = pltpu.VMEM((DEPTH, 9 * channels, channels), BF16)
    bias_room = pltpu.VMEM((DEPTH, DEPTH, EXTRA, channels), BF16)
    sems = pltpu.SemaphoreType.DMA((DEPTH, 2 * DEPTH))
    bias_sems = pltpu.SemaphoreType.DMA((DEPTH, DEPTH))
    params = pltpu.CompilerParams(vmem_limit_bytes=VMEM_LIMIT)

    def shaped(*shape):
        return jax.ShapeDtypeStruct(shape, BF16)

    cells = (across, channels)

    def flags_of(block):
        slot = (group - block) % groups
        slot = jnp.where(slot == 2, 3, jnp.where(slot == 3, 2, slot))
        return jnp.stack(
            [band == 0, band == band_count - 1, parity, turn, place, slot, block, group]
        ).astype(jnp.int32)

    forward = pl.pallas_call(
        forward_kernel,
        out_shape=(
            shaped(2 * rows + 2, *cells),
            shaped(groups, SLOPE_ROWS, *cells),
            shaped(DEPTH, *row_shape),
            shaped(groups, rows + 2, *cells),
            shaped(groups, rows + 2, *cells),
        ),
        in_specs=[smem, vmem, vmem, vmem] + [hbm] * 14,
        out_specs=(vmem,) + (hbm,) * 4,
        input_output_aliases={14: 1, 15: 2, 16: 3, 17: 4},
        scratch_shapes=[
            pltpu.VMEM((SLOPE_ROWS, *cells), BF16),
            pltpu.VMEM((DEPTH, *row_shape), BF16),
            wide,
            wide,
            weight_room,
            bias_room,
            sems,
            bias_sems,
            pltpu.SemaphoreType.DMA((4,)),
        ],
        compiler_params=params,
        name="forward",
    )
    backward = pl.pallas_call(
        backward_kernel,
        out_shape=(shaped(*row_shape), shaped(DEPTH, *row_shape)),
        in_specs=[smem] + [vmem] * 3 + [hbm] * 16,
        out_specs=(vmem, hbm),
        input_output_aliases={19: 1},
        scratch_shapes=[
            pltpu.VMEM((DEPTH, *row_shape), BF16),
            pltpu.VMEM((SLOPE_ROWS, *cells), BF16),
            pltpu.VMEM((rows + 2, *cells), BF16),
            pltpu.VMEM((rows + 2, *cells), BF16),
            pltpu.VMEM((3 * rows * across, channels), BF16),
            wide,
            pltpu.VMEM((3 * rows * across, channels), F32),
            weight_room,
            sems,
            pltpu.SemaphoreType.DMA((4,)),
        ],
        compiler_params=params,
        name="backward",
    )

    def forward_step(block, state):
        edge, outside, inside, *kept = state
        edge, *kept = forward(flags_of(block), edge, outside, inside, *mine, *theirs, *kept)
        return edge, *edges(edge), *kept

    room = pl.pallas_call(
        lambda *refs: None,
        out_shape=(
            shaped(groups, SLOPE_ROWS, *cells),
            shaped(DEPTH, *row_shape),
            shaped(groups, rows + 2, *cells),
            shaped(groups, rows + 2, *cells),
            shaped(DEPTH, *row_shape),
        ),
        out_specs=(hbm,) * 5,
        name="room",
    )()
    state = (edge, edge_outside, edge_inside, *room[:4])
    edge, last_outside, last_inside, slopes, states, far_outside, far_inside = lax.fori_loop(
        0, groups, forward_step, state
    )

    def sent(kept):
        received = [lax.dynamic_index_in_dim(kept, place, 0, keepdims=False)]
        for step in range(1, DEPTH):
            send = lax.dynamic_index_in_dim(kept, (place + step) % DEPTH, 0, keepdims=False)
            pairs = [(g * DEPTH + p, g * DEPTH + (p + step) % DEPTH) for g in range(groups) for p in range(DEPTH)]
            received.append(shift(send, "section", pairs))
        return received

    def set_in_order(places, *refs):
        out = refs[-1]
        for index, piece in enumerate(refs[:-1]):
            out[places[index]] = piece[...]

    def in_order(received):
        places = jnp.stack([(place - step) % DEPTH for step in range(DEPTH)]).astype(jnp.int32)
        return pl.pallas_call(
            set_in_order,
            out_shape=shaped(micro_count, *row_shape),
            in_specs=[smem] + [vmem] * DEPTH,
            out_specs=vmem,
            name="set_in_order",
        )(places, *received)[None]

    received = sent(states)

    def backward_step(step, state):
        upstream, above, below, grads = state
        block = groups - 1 - step
        upstream, grads = backward(
            flags_of(block), upstream, above, below, slopes, far_outside, far_inside, last_outside, last_inside,
            *mine, *theirs, grads,
        )
        above, below = lax.cond(block > 0, edges, lambda _: (above, below), upstream)
        return upstream, above, below, grads

    state = (upstream, start_outside, start_inside, room[4])
    grads = lax.fori_loop(0, groups, backward_step, state)[3]

    return in_order(received), in_order(sent(grads))


def solution(mesh):
    placed = (
        P(None, "band", None, None),
        P(None, "band", None, None),
        P("section", None, None, None, None),
        P("section", None),
    )
    return jax.shard_map(
        on_device,
        mesh=mesh,
        in_specs=placed,
        out_specs=(P("section", None, "band", None, None), P("section", None, "band", None, None)),
        check_vma=False,
    )
```

```python
import jax
import jax.numpy as jnp
from jax import lax
from jax.experimental import pallas as pl
from jax.experimental.pallas import tpu as pltpu
from jax.sharding import PartitionSpec as P


DEPTH = 4
CHUNKS = (1, 2)
EXTRA = 16
SLOPE_BASE = (0, 10, 18, 24)
SLOPE_ROWS = 28
VMEM_LIMIT = 52 * 1024 * 1024
BF16 = jnp.bfloat16
F32 = jnp.float32


def spread_columns(ref, base, value, shift, across, channels):
    count = value.shape[0]
    cells = value.reshape(count // across, across, channels)
    before = pltpu.roll(cells, shift % across, 1).reshape(count, channels)
    after = pltpu.roll(cells, -shift % across, 1).reshape(count, channels)
    ref[pl.ds(base, count), 0:channels] = before.astype(BF16)
    ref[pl.ds(base, count), channels : 2 * channels] = value.astype(BF16)
    ref[pl.ds(base, count), 2 * channels : 3 * channels] = after.astype(BF16)


def copy_weights(flags, mine, theirs, weights, bias, sems, bias_sems, order):
    rows = weights.shape[1] // (2 * DEPTH)
    slot = flags[5]
    turn = flags[3]
    behind = (0, 1, 3, 2)

    def start(parity, place, layer):
        away = behind.index((place - layer) % DEPTH)
        for side, pieces in enumerate((mine, theirs)):
            core = parity if side == 0 else 1 - parity
            for other in range(DEPTH):
                outer, inner = (other, away) if core == 0 else (away, other)
                source = pieces[outer] if outer < 3 else pieces[3 + inner // 2]
                index = inner if outer < 3 else inner % 2
                at = core * DEPTH + (turn - behind[other] + DEPTH) % DEPTH
                pltpu.make_async_copy(
                    source.at[index, slot, pl.ds(0, rows)],
                    weights.at[layer, pl.ds(pl.multiple_of(at * rows, 32), rows)],
                    sems.at[layer, at],
                ).start()
                if bias is not None and side == 0 and other == 0:
                    pltpu.make_async_copy(
                        source.at[index, slot, pl.ds(rows, EXTRA)], bias.at[layer], bias_sems.at[layer]
                    ).start()

    for parity in range(2):
        for place in range(DEPTH):

            @pl.when((flags[2] == parity) & (flags[4] == place))
            def _(parity=parity, place=place):
                for layer in order:
                    start(parity, place, layer)

    def wait(layer):
        for at in range(2 * DEPTH):
            pltpu.make_async_copy(
                mine[0].at[0, 0, pl.ds(0, rows)], weights.at[layer, pl.ds(at * rows, rows)], sems.at[layer, at]
            ).wait()
        if bias is not None:
            pltpu.make_async_copy(mine[0].at[0, 0, pl.ds(rows, EXTRA)], bias.at[layer], bias_sems.at[layer]).wait()

    return wait


def forward_kernel(flags, own, outside, inside, *refs):
    mine, theirs = refs[:5], refs[5:10]
    edge, all_slopes, kept_states, all_outside, all_inside = refs[14:19]
    slopes, states, wide, other, weights, bias, sems, bias_sems, out_sems = refs[19:]
    block, group = flags[6], flags[7]
    save = pltpu.make_async_copy(slopes, all_slopes.at[block], out_sems.at[0])
    keep = pltpu.make_async_copy(states, kept_states, out_sems.at[1])
    rows, across, channels = states.shape[1:]
    wait = copy_weights(flags, mine, theirs, weights, bias, sems, bias_sems, range(DEPTH))
    last_block = (block + DEPTH - 1) % DEPTH
    pass_on = [
        pltpu.make_async_copy(piece.at[pl.ds(rows, rows + 2)], kept.at[last_block], out_sems.at[2 + index])
        for index, (piece, kept) in enumerate(((outside, all_outside), (inside, all_inside)))
    ]
    for copy in pass_on:
        copy.start()
    odd = flags[2] == 1
    for part in range(3):

        @pl.loop(0, rows, unroll=2)
        def _(row, part=part):
            base = pl.multiple_of((part * rows + row) * across, across)
            if part == 1:
                line = own[row].astype(F32)
            else:
                pair = (inside, outside) if part == 0 else (outside, inside)
                line = jnp.where(odd, pair[0][row].astype(F32), pair[1][row].astype(F32))
            spread_columns(wide, base, line, 1, across, channels)

    def poles(ref):
        middle = across // 2
        top, bottom = rows * across, (2 * rows - 1) * across

        @pl.when(flags[0] == 1)
        def _():
            ref[top - across : top - middle, :] = ref[top + middle : top + across, :]
            ref[top - middle : top, :] = ref[top : top + middle, :]

        @pl.when(flags[1] == 1)
        def _():
            ref[bottom + across : bottom + across + middle, :] = ref[bottom + middle : bottom + across, :]
            ref[bottom + across + middle : bottom + 2 * across, :] = ref[bottom : bottom + middle, :]

    for layer in range(DEPTH):
        source, target = (wide, other) if layer % 2 == 0 else (other, wide)
        poles(source)
        wait(layer)
        reach = DEPTH - 1 - layer
        parts = bias[layer].astype(F32)
        offset = (parts[0:1] + parts[1:2]) + parts[2:3]

        height = rows + 2 * reach
        for index in range(0, height, CHUNKS[0]):
            count = min(CHUNKS[0], height - index)
            step = count * across
            base = (rows - reach + index) * across
            preact = None
            for tap in range(3):
                term = jnp.dot(
                    source[pl.ds(base + (tap - 1) * across, step), :],
                    weights[layer, tap * 3 * channels : (tap + 1) * 3 * channels, :],
                    preferred_element_type=F32,
                )
                preact = term if preact is None else preact + term
            preact = preact + offset
            sigmoid = 0.5 * jnp.tanh(0.5 * preact) + 0.5
            silu = preact * sigmoid
            slope = (sigmoid + silu * (1.0 - sigmoid)).astype(BF16).reshape(count, across, channels)
            before = source[pl.ds(base, step), channels : 2 * channels].astype(F32)
            result = (before + silu).astype(BF16)
            if layer < DEPTH - 1:
                spread_columns(target, base, result.astype(F32), 1, across, channels)
            slopes[pl.ds(SLOPE_BASE[layer] + index, count)] = slope
            if layer == DEPTH - 1:
                edge[pl.ds(index, count)] = result.reshape(count, across, channels)

        if layer < DEPTH - 1:
            own_cells = target[rows * across : 2 * rows * across, channels : 2 * channels]
            states[layer] = own_cells.reshape(rows, across, channels)
    states[DEPTH - 1] = edge[0:rows]
    edge[rows : 2 * rows] = slopes[SLOPE_BASE[3] : SLOPE_BASE[3] + rows]
    edge[2 * rows :] = slopes[SLOPE_BASE[2] + 2 : SLOPE_BASE[2] + 4]
    save.start()

    @pl.when(block == group)
    def _():
        keep.start()
        keep.wait()

    for copy in [save] + pass_on:
        copy.wait()


def backward_kernel(flags, own, outside, inside, all_slopes, all_outside, all_inside, last_outside, last_inside, *refs):
    mine, theirs = refs[:5], refs[5:10]
    rows = own.shape[0]
    current, kept_grads = refs[11:13]
    grads, slopes, far_above, far_below, upstream, wide, added, weights, sems, out_sems = refs[13:]
    block, group = flags[6], flags[7]
    odd = flags[2] == 1
    for swapped in range(2):

        @pl.when((flags[2] == swapped) & (block < DEPTH - 1))
        def _(swapped=swapped):
            ends = (all_inside, all_outside) if swapped else (all_outside, all_inside)
            for index, (source, target) in enumerate(zip(ends, (far_above, far_below))):
                pltpu.make_async_copy(source.at[block], target, out_sems.at[index]).start()

        @pl.when((flags[2] == swapped) & (block == DEPTH - 1))
        def _(swapped=swapped):
            ends = (last_inside, last_outside) if swapped else (last_outside, last_inside)
            for index, (source, target) in enumerate(zip(ends, (far_above, far_below))):
                pltpu.make_async_copy(source.at[pl.ds(rows, rows + 2)], target, out_sems.at[index]).start()

    pltpu.make_async_copy(all_slopes.at[block], slopes, out_sems.at[2]).start()
    loads = [
        pltpu.make_async_copy(source.at[block], target, out_sems.at[index])
        for index, (source, target) in enumerate(
            ((all_outside, far_above), (all_inside, far_below), (all_slopes, slopes))
        )
    ]
    keep = pltpu.make_async_copy(grads, kept_grads, out_sems.at[3])
    rows, across, channels = own.shape
    middle = across // 2
    wait = copy_weights(flags, mine, theirs, weights, None, sems, None, tuple(reversed(range(DEPTH))))
    for row in range(rows):
        lines = outside[row], inside[row]
        for part, line in enumerate((jnp.where(odd, lines[1], lines[0]), own[row], jnp.where(odd, lines[0], lines[1]))):
            at = (part * rows + row) * across
            upstream[at : at + across] = line
    added[...] = jnp.zeros(added.shape, F32)
    for load in loads:
        load.wait()
    contract = (((1,), (1,)), ((), ()))

    def tap_weight(layer, tap, column):
        at = (tap * 3 + column) * channels
        return weights[layer, at : at + channels, :]

    for layer in reversed(range(DEPTH)):

        def deltas(first, count, slope_ref, slope_base):
            @pl.loop(0, count, unroll=2)
            def _(index):
                base = pl.multiple_of((first + index) * across, across)
                delta = upstream[pl.ds(base, across)].astype(F32) * slope_ref[slope_base + index].astype(F32)
                spread_columns(wide, base, delta.astype(BF16).astype(F32), -1, across, channels)

        if layer == 3:
            deltas(0, rows, far_above, 0)
            deltas(rows, rows, slopes, SLOPE_BASE[3])
            deltas(2 * rows, rows, far_below, 0)
        elif layer == 2:
            deltas(1, 2, far_above, rows)
            deltas(rows - 1, rows + 2, slopes, SLOPE_BASE[2])
            deltas(2 * rows + 1, 2, far_below, rows)
        else:
            deltas(rows - 1 - layer, rows + 2 + 2 * layer, slopes, SLOPE_BASE[layer] + (2 if layer == 0 else 0))
        top, bottom = rows * across, (2 * rows - 1) * across
        wait(layer)

        def edge_terms(base, tap, layer=layer):
            for piece in range(2):
                start = base + (1 - piece) * middle
                total = None
                for column in range(3):
                    term = lax.dot_general(
                        wide[start : start + middle, column * channels : (column + 1) * channels],
                        tap_weight(layer, tap, column), contract, preferred_element_type=F32,
                    )
                    total = term if total is None else total + term
                added[base + piece * middle : base + (piece + 1) * middle, :] = total

        @pl.when(flags[0] == 1)
        def _():
            wide[top - across : top, :] = jnp.zeros((across, 3 * channels), BF16)
            edge_terms(top, 0)

        @pl.when(flags[1] == 1)
        def _():
            wide[bottom + across : bottom + 2 * across, :] = jnp.zeros((across, 3 * channels), BF16)
            edge_terms(bottom, 2)

        height = rows + 2 * layer
        for index in range(0, height, CHUNKS[1]):
            count = min(CHUNKS[1], height - index)
            step = count * across
            base = (rows - layer + index) * across
            total = upstream[pl.ds(base, step)].astype(F32) + added[pl.ds(base, step)]
            for tap in range(3):
                for column in range(3):
                    total = total + lax.dot_general(
                        wide[pl.ds(base + (1 - tap) * across, step), column * channels : (column + 1) * channels],
                        tap_weight(layer, tap, column), contract, preferred_element_type=F32,
                    )
            upstream[pl.ds(base, step)] = total.astype(BF16)

        grads[layer] = upstream[rows * across : 2 * rows * across].reshape(rows, across, channels)
    current[...] = grads[0]

    @pl.when(block == group)
    def _():
        keep.start()
        keep.wait()


def shift(block, axis, pairs):
    return lax.ppermute(block, axis, pairs)


def on_device(fields, cotangent, kernels, biases):
    band_count = lax.axis_size("band")
    section_count = lax.axis_size("section")
    micro_count, rows, across, channels = fields.shape
    groups = section_count // DEPTH
    band = lax.axis_index("band")
    section = lax.axis_index("section")
    group = section // DEPTH
    place = section % DEPTH
    parity = band % 2
    turn = band // 2 % DEPTH
    bias = biases[0]
    high = lax.reduce_precision(bias, 8, 7)
    middle = lax.reduce_precision(bias - high, 8, 7)
    low = bias - high - middle
    extra = jnp.stack([high, middle, low] + [jnp.zeros_like(bias)] * (EXTRA - 3)).astype(BF16)

    def route(move):
        pairs = []
        for b in range(band_count):
            for s in range(section_count):
                low, y, core, z, x = b // (2 * DEPTH), b // 2 % DEPTH, b % 2, s // DEPTH, s % DEPTH
                y, core, z, x = move(y, core, z, x)
                to = (low * 2 * DEPTH + y % DEPTH * 2 + core) * section_count + z % DEPTH * DEPTH + x % DEPTH
                pairs.append((b * section_count + s, to))
        return pairs

    def carry(block, pairs):
        return lax.ppermute(block, ("band", "section"), pairs)

    def around(block, forth, back):
        middle = block.shape[0] // 2
        behind, ahead = carry(block, route(forth)), carry(block, route(back))
        return behind, ahead, carry(behind[:middle], route(forth)), carry(ahead[middle:], route(back))

    def joined(block, forth, back):
        behind, ahead, low, high = around(block, forth, back)
        return jnp.stack([block, behind, ahead, jnp.concatenate([low, high])])

    outside = [pair for i in range(1, band_count - 1, 2) for pair in ((i, i + 1), (i + 1, i))]

    partner = [(i, i ^ 1) for i in range(band_count)]

    def edges(block):
        return shift(block, "band", outside), shift(block, "band", partner)

    current, upstream = (lax.dynamic_index_in_dim(block, place, 0, keepdims=False) for block in (fields, cotangent))
    edge = jnp.concatenate([current, upstream, upstream[:2]])

    quarter = 9 * channels // 2 // DEPTH
    start = (parity * DEPTH + turn) * quarter
    piece = lax.dynamic_slice_in_dim(kernels.reshape(9 * channels, channels), start, quarter, 0)
    piece = jnp.concatenate([piece, extra])
    hbm = pl.BlockSpec(memory_space=pl.ANY)
    vmem = pl.BlockSpec(memory_space=pltpu.VMEM)
    edge_outside, edge_inside = edges(edge)
    piece = joined(piece, lambda y, c, z, x: (y, c, z + 1, x), lambda y, c, z, x: (y, c, z - 1, x))

    def take_edges(piece, outside, inside, out, first, second):
        first[...] = outside[rows : 2 * rows]
        second[...] = inside[rows : 2 * rows]

    part_shape = jax.ShapeDtypeStruct((rows, across, channels), BF16)
    piece, start_outside, start_inside = pl.pallas_call(
        take_edges,
        out_shape=(jax.ShapeDtypeStruct(piece.shape, BF16), part_shape, part_shape),
        in_specs=[hbm, vmem, vmem],
        out_specs=(hbm, vmem, vmem),
        input_output_aliases={0: 0},
        name="take_edges",
    )(piece, edge_outside, edge_inside)
    piece = joined(
        piece,
        lambda y, c, z, x: (y + c, c, z, x + 1 - c),
        lambda y, c, z, x: (y - c, c, z, x - 1 + c),
    )
    ring = around(
        piece,
        lambda y, c, z, x: (y + 1 - c, c, z, x + c),
        lambda y, c, z, x: (y - 1 + c, c, z, x - c),
    )
    mine = (piece,) + ring
    theirs = tuple(carry(block, route(lambda y, c, z, x: (y, 1 - c, z, x))) for block in mine)

    row_shape = (rows, across, channels)
    smem = pl.BlockSpec(memory_space=pltpu.SMEM)
    vmem = pl.BlockSpec(memory_space=pltpu.VMEM)
    hbm = pl.BlockSpec(memory_space=pl.ANY)
    wide = pltpu.VMEM((3 * rows * across, 3 * channels), BF16)
    weight_room = pltpu.VMEM((DEPTH, 9 * channels, channels), BF16)
    bias_room = pltpu.VMEM((DEPTH, EXTRA, channels), BF16)
    sems = pltpu.SemaphoreType.DMA((DEPTH, 2 * DEPTH))
    bias_sems = pltpu.SemaphoreType.DMA((DEPTH,))
    params = pltpu.CompilerParams(vmem_limit_bytes=VMEM_LIMIT)

    def shaped(*shape):
        return jax.ShapeDtypeStruct(shape, BF16)

    cells = (across, channels)

    def flags_of(block):
        slot = (group - block) % groups
        slot = jnp.where(slot == 2, 3, jnp.where(slot == 3, 2, slot))
        return jnp.stack(
            [band == 0, band == band_count - 1, parity, turn, place, slot, block, group]
        ).astype(jnp.int32)

    forward = pl.pallas_call(
        forward_kernel,
        out_shape=(
            shaped(2 * rows + 2, *cells),
            shaped(groups, SLOPE_ROWS, *cells),
            shaped(DEPTH, *row_shape),
            shaped(groups, rows + 2, *cells),
            shaped(groups, rows + 2, *cells),
        ),
        in_specs=[smem, vmem, vmem, vmem] + [hbm] * 14,
        out_specs=(vmem,) + (hbm,) * 4,
        input_output_aliases={14: 1, 15: 2, 16: 3, 17: 4},
        scratch_shapes=[
            pltpu.VMEM((SLOPE_ROWS, *cells), BF16),
            pltpu.VMEM((DEPTH, *row_shape), BF16),
            wide,
            wide,
            weight_room,
            bias_room,
            sems,
            bias_sems,
            pltpu.SemaphoreType.DMA((4,)),
        ],
        compiler_params=params,
        name="forward",
    )
    backward = pl.pallas_call(
        backward_kernel,
        out_shape=(shaped(*row_shape), shaped(DEPTH, *row_shape)),
        in_specs=[smem] + [vmem] * 3 + [hbm] * 16,
        out_specs=(vmem, hbm),
        input_output_aliases={19: 1},
        scratch_shapes=[
            pltpu.VMEM((DEPTH, *row_shape), BF16),
            pltpu.VMEM((SLOPE_ROWS, *cells), BF16),
            pltpu.VMEM((rows + 2, *cells), BF16),
            pltpu.VMEM((rows + 2, *cells), BF16),
            pltpu.VMEM((3 * rows * across, channels), BF16),
            wide,
            pltpu.VMEM((3 * rows * across, channels), F32),
            weight_room,
            sems,
            pltpu.SemaphoreType.DMA((4,)),
        ],
        compiler_params=params,
        name="backward",
    )

    def forward_step(block, state):
        edge, outside, inside, *kept = state
        edge, *kept = forward(flags_of(block), edge, outside, inside, *mine, *theirs, *kept)
        return edge, *edges(edge), *kept

    room = pl.pallas_call(
        lambda *refs: None,
        out_shape=(
            shaped(groups, SLOPE_ROWS, *cells),
            shaped(DEPTH, *row_shape),
            shaped(groups, rows + 2, *cells),
            shaped(groups, rows + 2, *cells),
            shaped(DEPTH, *row_shape),
        ),
        out_specs=(hbm,) * 5,
        name="room",
    )()
    state = (edge, edge_outside, edge_inside, *room[:4])
    edge, last_outside, last_inside, slopes, states, far_outside, far_inside = lax.fori_loop(
        0, groups, forward_step, state
    )

    def sent(kept):
        received = [lax.dynamic_index_in_dim(kept, place, 0, keepdims=False)]
        for step in range(1, DEPTH):
            send = lax.dynamic_index_in_dim(kept, (place + step) % DEPTH, 0, keepdims=False)
            pairs = [(g * DEPTH + p, g * DEPTH + (p + step) % DEPTH) for g in range(groups) for p in range(DEPTH)]
            received.append(shift(send, "section", pairs))
        return received

    def set_in_order(places, *refs):
        out = refs[-1]
        for index, piece in enumerate(refs[:-1]):
            out[places[index]] = piece[...]

    def in_order(received):
        places = jnp.stack([(place - step) % DEPTH for step in range(DEPTH)]).astype(jnp.int32)
        return pl.pallas_call(
            set_in_order,
            out_shape=shaped(micro_count, *row_shape),
            in_specs=[smem] + [vmem] * DEPTH,
            out_specs=vmem,
            name="set_in_order",
        )(places, *received)[None]

    received = sent(states)

    def backward_step(step, state):
        upstream, above, below, grads = state
        block = groups - 1 - step
        upstream, grads = backward(
            flags_of(block), upstream, above, below, slopes, far_outside, far_inside, last_outside, last_inside,
            *mine, *theirs, grads,
        )
        above, below = lax.cond(block > 0, edges, lambda _: (above, below), upstream)
        return upstream, above, below, grads

    state = (upstream, start_outside, start_inside, room[4])
    grads = lax.fori_loop(0, groups, backward_step, state)[3]

    return in_order(received), in_order(sent(grads))


def solution(mesh):
    placed = (
        P(None, "band", None, None),
        P(None, "band", None, None),
        P("section", None, None, None, None),
        P("section", None),
    )
    return jax.shard_map(
        on_device,
        mesh=mesh,
        in_specs=placed,
        out_specs=(P("section", None, "band", None, None), P("section", None, "band", None, None)),
        check_vma=False,
    )
```
